256 devices in a mesh: dp: 16 (over y, x), expert: 16 (over z, core).
Axes of the slice: x: 4, y: 4, z: 8, core: 2. Of those that a mesh axis runs over, the one named last changes fastest.
Arguments:
- tokens: bfloat16 [32768, 1024], P(('dp', 'expert')), may hold values from -6 to 6
- cotangent: bfloat16 [32768, 1024], P(('dp', 'expert')), may hold values from -6 to 6
- expert_ids: int32 [32768, 8], P(('dp', 'expert')), may hold values from 0 to 31, all different within a row; in each aligned block of 128 rows (0 to 127, 128 to 255, ...) at most 40 rows name the same one
- gate_probs: bfloat16 [32768, 8], P(('dp', 'expert')), may hold values from 0.049804688 to 0.5
- gate_up: bfloat16 [32, 1024, 1024], P('expert', 'dp'), may hold values from -0.1875 to 0.1875
- down_proj: bfloat16 [32, 512, 1024], P('expert', 'dp'), may hold values from -0.25 to 0.25
Outputs:
- grad_tokens: bfloat16 [32768, 1024], P(('dp', 'expert'))
- grad_gates: bfloat16 [32768, 8], P(('dp', 'expert'))
- grad_gate_up: float32 [32, 1024, 1024], P('expert', 'dp')
- grad_down: float32 [32, 512, 1024], P('expert', 'dp')
The draws below stay inside these ranges and needn't reach their ends.
Inputs may be any that keep to these rules, and one draw needn't show every extreme that they name: `expert_ids`: each token names 8 different experts. Among the 128 tokens of one device (aligned blocks of rows) no expert is named more than 40 times, and in every draw some expert is named exactly 40 times by the tokens of some device.
All inputs are finite; a program needn't handle non-finite values.
Results may differ from the reference program's by a relative error of at most 0.0058.
Values may be sent and summed in bfloat16 or wider, within the bound.
No kernel may reach another device: no remote copies, remote signals or barrier semaphores. Data moves between devices by JAX's collectives and lax.ppermute only.
A program may use at most 128 MiB of HBM per device.

```python
import math
import jax
import jax.numpy as jnp
import numpy as np
from jax import lax

D = 1024
F = 512
TOP = 8
TOK_DEV = 128
EXPERTS = 32
CAP = 40
TOKENS = 32768


def block_levels(key, dims, split, least, largest):
    gain = 1.0
    for dim, blocks in split:
        steps = jax.random.uniform(jax.random.fold_in(jax.random.fold_in(key, 6), dim), (blocks,), jnp.float32, least / len(split), largest / len(split))
        gain = gain * jnp.repeat(jnp.exp(steps), dims[dim] // blocks).reshape((-1,) + (1,) * (len(dims) - 1 - dim))
    return gain


def assign_block(key, own, number, rows, amount, top, bound, slope):
    ranking = jax.random.permutation(key, amount)
    heavy_load, ordinary = shares(amount, rows * top, bound, slope, True), shares(amount, rows * top, bound, slope, False)
    places = jnp.arange(amount)

    def named(lengths, turn):
        used = int((lengths > 0).sum())
        fixed = max(1, used // 4)
        moved = fixed + (places - fixed + turn * (used - fixed)) % max(1, amount - fixed)
        return jnp.zeros((amount,), jnp.int32).at[ranking[jnp.where(places < fixed, places, moved)]].set(jnp.asarray(lengths, jnp.int32))

    lengths = jnp.where(number % 4 == 0, named(heavy_load, number // 4), named(ordinary, number - number // 4 - 1))
    mixed = jax.random.permutation(jax.random.fold_in(own, 3), amount)
    donor, taker = mixed[0:amount // 2 * 2:2], mixed[1:amount // 2 * 2:2]
    margin = jnp.minimum(lengths[donor] - 1, bound - lengths[taker]) // 2
    margin = jnp.where((donor == ranking[0]) | (taker == ranking[0]) | (lengths[taker] == 0), 0, jnp.maximum(margin, 0))
    moved = jax.random.randint(jax.random.fold_in(own, 4), (amount // 2,), 0, 1 << 20) % (margin + 1)
    lengths = lengths.at[donor].add(-moved).at[taker].add(moved)
    labels = jnp.searchsorted(jnp.cumsum(lengths), jnp.arange(rows * top), side="right").astype(jnp.int32)
    listing = labels.reshape(top, rows).T
    listing = listing[jax.random.permutation(jax.random.fold_in(own, 1), rows)]
    turn = jax.random.randint(jax.random.fold_in(own, 2), (rows, 1), 0, top)
    return jnp.take_along_axis(listing, (jnp.arange(top)[None, :] + turn) % top, axis=1)


def shares(amount, total, limit, lean, full):
    loads = [(1 << 20) // math.isqrt(grade ** lean) + 1 for grade in range(1, amount + 1)]
    largest = limit if full else min(limit, max(-(-total // amount), total * loads[0] // sum(loads)))
    least = 1 if total - largest >= amount - 1 else 0
    given, rest = [largest] + [least] * (amount - 1), total - largest - least * (amount - 1)
    while rest > 0:
        movable = [i for i in range(1, amount) if given[i] < largest] or [i for i in range(1, amount) if given[i] < limit]
        pool, remaining = sum([loads[i] for i in movable]), rest
        for i in movable:
            more = min(limit - given[i], max(1, remaining * loads[i] // pool), rest)
            given[i] = given[i] + more
            rest = rest - more
    return np.array(given)


def noise(key, dims, scale, limit, split=(), held_as=jnp.bfloat16):
    values = jax.random.normal(key, dims, jnp.float32) * scale
    if len(split) > 0:
        values = block_levels(key, dims, split, -0.22, 0.18) * values
    return jnp.clip(values, min=-limit, max=limit).astype(held_as)


def setup_inputs(seed: int = 0) -> dict:
    keys = jax.random.split(jax.random.key(seed), 7)
    tokens = noise(keys[0], (TOKENS, D), 1.0, 6.0, ((0, 256),))
    cotangent = noise(keys[1], (TOKENS, D), 1.0, 6.0, ((0, 256),))
    expert_ids_keys = jax.random.split(jax.random.fold_in(keys[2], 1), TOKENS // TOK_DEV)
    expert_ids_turns = jax.random.permutation(jax.random.fold_in(keys[2], 3), TOKENS // TOK_DEV)
    expert_ids = jax.vmap(lambda own, number: assign_block(jax.random.fold_in(keys[2], 2), own, number, TOK_DEV, EXPERTS, TOP, CAP, 1))(expert_ids_keys, expert_ids_turns).reshape((TOKENS, TOP))
    gate_probs = jnp.clip(0.049804688 + 0.4501953 * jax.random.uniform(keys[3], (TOKENS, TOP), jnp.float32) ** block_levels(keys[3], (TOKENS, TOP), ((0, 256),), -0.2, 0.2), 0.049804688, 0.5).astype(jnp.bfloat16)
    gate_up = noise(keys[4], (EXPERTS, D, 2 * F), D ** -0.5, 0.1875, ((0, 16), (1, 16)))
    down_proj = noise(keys[5], (EXPERTS, F, D), F ** -0.5, 0.25, ((0, 16), (1, 16)))
    return dict(tokens=tokens, cotangent=cotangent, expert_ids=expert_ids, gate_probs=gate_probs, gate_up=gate_up, down_proj=down_proj)


def expert_grads(routed_x, routed_dy, routed_gate, w_in, w_out):
    pre_act = jnp.dot(routed_x, w_in, preferred_element_type=jnp.float32)
    hidden = w_out.shape[0]
    gate_pre = pre_act[:, :hidden]
    up_pre = pre_act[:, hidden:]
    sigmoid_h = jax.nn.sigmoid(gate_pre)
    silu_h = gate_pre * sigmoid_h
    activation = silu_h * up_pre
    raw_grad = jnp.dot(routed_dy, w_out.T, preferred_element_type=jnp.float32)
    gate_col = routed_gate.astype(jnp.float32)[:, None]
    act_grad = gate_col * raw_grad
    grad_gate = act_grad * up_pre * sigmoid_h * (1.0 + gate_pre * (1.0 - sigmoid_h))
    grad_up = act_grad * silu_h
    pre_grad = jnp.concatenate([grad_gate, grad_up], axis=-1).astype(jnp.bfloat16)
    scaled_act = (gate_col * activation).astype(jnp.bfloat16)
    slot_dx = jnp.dot(pre_grad, w_in.T, preferred_element_type=jnp.float32).astype(jnp.bfloat16)
    slot_gate = jnp.sum(activation * raw_grad, axis=-1).astype(jnp.bfloat16)
    return pre_grad, scaled_act, slot_dx, slot_gate


def reference(tokens, cotangent, expert_ids, gate_probs, gate_up, down_proj):
    tok_total, width = tokens.shape
    devices_all = tok_total // TOK_DEV
    per_device = TOK_DEV * TOP
    assign_total = tok_total * TOP
    flat_ids = expert_ids.reshape(devices_all, per_device).astype(jnp.int32)
    onehot = (flat_ids[:, :, None] == jnp.arange(EXPERTS, dtype=jnp.int32)[None, None, :]).astype(jnp.int32)
    before = jnp.cumsum(onehot, axis=1) - onehot
    slot_rank = jnp.sum(before * onehot, axis=2).astype(jnp.int32)
    device_row = jnp.arange(devices_all, dtype=jnp.int32)[:, None]
    column = (device_row * CAP + slot_rank).astype(jnp.int32)
    assigned_all = jnp.arange(assign_total, dtype=jnp.int32).reshape(devices_all, per_device)
    table = jnp.full((EXPERTS, devices_all * CAP), assign_total, jnp.int32).at[flat_ids, column].set(assigned_all)
    flat_gates = gate_probs.reshape(-1)

    def one_expert(carry, inputs):
        grad_acc, gate_acc = carry
        assigned, w_in, w_out = inputs
        valid = assigned < assign_total
        safe_assign = jnp.where(valid, assigned, 0).astype(jnp.int32)
        token_of = (safe_assign // TOP).astype(jnp.int32)
        routed_x = jnp.where(valid[:, None], tokens[token_of], jnp.zeros((), jnp.bfloat16)).astype(jnp.bfloat16)
        routed_dy = jnp.where(valid[:, None], cotangent[token_of], jnp.zeros((), jnp.bfloat16)).astype(jnp.bfloat16)
        routed_gate = jnp.where(valid, flat_gates[safe_assign], jnp.zeros((), jnp.bfloat16)).astype(jnp.bfloat16)
        pre_grad, scaled_act, slot_dx, slot_gate = expert_grads(routed_x, routed_dy, routed_gate, w_in, w_out)
        grad_in = jnp.dot(routed_x.T, pre_grad, preferred_element_type=jnp.float32)
        grad_out = jnp.dot(scaled_act.T, routed_dy, preferred_element_type=jnp.float32)
        target = jnp.where(valid, token_of, tok_total).astype(jnp.int32)
        grad_acc = grad_acc.at[target].add(slot_dx.astype(jnp.float32), mode="drop")
        gate_acc = gate_acc.at[assigned].set(slot_gate.astype(jnp.float32), mode="drop")
        return (grad_acc, gate_acc), (grad_in, grad_out)

    start = (jnp.zeros((tok_total, width), jnp.float32), jnp.zeros((assign_total,), jnp.float32))
    (grad_acc, gate_acc), (grad_gate_up, grad_down) = lax.scan(one_expert, start, (table, gate_up, down_proj))
    grad_tokens = grad_acc.astype(jnp.bfloat16)
    grad_gates = gate_acc.reshape(tok_total, TOP).astype(jnp.bfloat16)
    return grad_tokens, grad_gates, grad_gate_up, grad_down
```

```python
import functools

import jax
import jax.numpy as jnp
from jax import lax
from jax.experimental import pallas as pl
from jax.experimental.pallas import tpu as pltpu
from jax.sharding import Mesh
from jax.sharding import PartitionSpec as P

BF16 = jnp.bfloat16
F32 = jnp.float32
TOP = 8
CAP = 40
TOK = 128
WIDTH = 1024
HID = 512
ROWS_IN = 64
ROWS_OUT = 32
ROWS = ROWS_IN + ROWS_OUT
CHIPS = 8
PAIR = 2 * CAP
SLOTS = CHIPS * PAIR
VMEM_LIMIT = 60 * 1024 * 1024

UP = [(i, (i + 1) % 4) for i in range(4)]
DOWN = [(i, (i - 1) % 4) for i in range(4)]


def dot(a, b, dims):
    return lax.dot_general(a, b, (dims, ((), ())), preferred_element_type=F32)


NN = ((1,), (0,))
NT = ((1,), (1,))
TN = ((0,), (0,))


def route_kernel(first_ref, pay_ref, x_ref, dy_ref, gate_ref, sel_ref):
    first = first_ref[0]
    upper = (
        lax.broadcasted_iota(jnp.int32, (TOK, TOK), 0)
        < lax.broadcasted_iota(jnp.int32, (TOK, TOK), 1)
    ).astype(BF16)
    named, weights = [], []
    for e in range(2):
        expert = (first + e).astype(F32)
        for c in range(2):
            ids = pay_ref[c, 2 * TOK : 2 * TOK + TOP, 0:TOK].astype(F32)
            probs = pay_ref[c, 2 * TOK : 2 * TOK + TOP, TOK : 2 * TOK].astype(F32)
            hit = jnp.where(ids == expert, 1.0, 0.0)
            named.append(jnp.sum(hit, axis=0, keepdims=True))
            weights.append(jnp.sum(hit * probs, axis=0, keepdims=True))
    marks = jnp.concatenate(named + named, axis=0)
    ranks = dot(marks.astype(BF16), upper, NN)
    slot = lax.broadcasted_iota(jnp.int32, (PAIR, TOK), 0).astype(F32)
    picks = []
    for e in range(2):
        halves = []
        for c in range(2):
            i = 2 * e + c
            place = jnp.where(marks[i : i + 1] > 0.5, ranks[i : i + 1] + float(CAP * c), -1.0)
            halves.append(jnp.where(slot == place, 1.0, 0.0))
        pick = jnp.concatenate(halves, axis=1)
        prob = jnp.concatenate([weights[2 * e], weights[2 * e + 1]], axis=1)
        column = jnp.sum(pick * prob, axis=1, keepdims=True)
        gate_ref[e] = jnp.broadcast_to(column, (PAIR, TOK))
        picks.append(pick)
    sel = jnp.concatenate(picks, axis=0).astype(BF16)
    sel_ref[0] = sel
    x = jnp.concatenate([pay_ref[0, 0:TOK], pay_ref[1, 0:TOK]], axis=0)
    routed = dot(sel, x, NN).astype(BF16)
    x_ref[0] = routed[:PAIR]
    x_ref[1] = routed[PAIR:]
    dy = jnp.concatenate([pay_ref[0, TOK : 2 * TOK], pay_ref[1, TOK : 2 * TOK]], axis=0)
    routed = dot(sel, dy, NN).astype(BF16)
    dy_ref[0] = routed[:PAIR]
    dy_ref[1] = routed[PAIR:]


def route(first, pay):
    return pl.pallas_call(
        route_kernel,
        name="route",
        grid_spec=pltpu.PrefetchScalarGridSpec(
            num_scalar_prefetch=1,
            grid=(CHIPS,),
            in_specs=[pl.BlockSpec((2, 2 * TOK + TOP, WIDTH), lambda p, f: (p, 0, 0))],
            out_specs=[
                pl.BlockSpec((2, PAIR, WIDTH), lambda p, f: (0, p, 0)),
                pl.BlockSpec((2, PAIR, WIDTH), lambda p, f: (0, p, 0)),
                pl.BlockSpec((2, PAIR, TOK), lambda p, f: (0, p, 0)),
                pl.BlockSpec((1, 2 * PAIR, 2 * TOK), lambda p, f: (p, 0, 0)),
            ],
        ),
        out_shape=[
            jax.ShapeDtypeStruct((2, SLOTS, WIDTH), BF16),
            jax.ShapeDtypeStruct((2, SLOTS, WIDTH), BF16),
            jax.ShapeDtypeStruct((2, SLOTS, TOK), F32),
            jax.ShapeDtypeStruct((CHIPS, 2 * PAIR, 2 * TOK), BF16),
        ],
        compiler_params=pltpu.CompilerParams(vmem_limit_bytes=VMEM_LIMIT),
        cost_estimate=pl.CostEstimate(
            flops=4 * 1024 * 1280 * 1024, bytes_accessed=14_000_000, transcendentals=0
        ),
    )(first, pay)


def expert_kernel(
    inner_first,
    place_ref,
    x_ref,
    dy_ref,
    gate_ref,
    own_ref,
    from_down_ref,
    from_up_ref,
    far_a_ref,
    far_b_ref,
    g_far_a,
    g_far_b,
    g_up,
    g_dn,
    g_own,
    dx_ref,
    sg_ref,
    w_in,
    w_out,
    pre,
    act,
    xt,
    at,
    grads,
    wsem,
    gsem,
):
    my_outer = place_ref[0]
    my_inner = place_ref[1]

    def block_of(outer, inner):
        return inner * 4 + outer if inner_first else outer * 4 + inner

    loads = []
    n = 0
    for oj in range(4):
        for ij in range(4):
            if oj == 0:
                src = own_ref.at[ij]
            elif oj == 1:
                src = from_down_ref.at[ij]
            elif oj == 3:
                src = from_up_ref.at[ij]
            elif ij < 2:
                src = far_a_ref.at[ij]
            else:
                src = far_b_ref.at[ij - 2]
            outer = lax.rem(my_outer + 4 - oj, 4)
            inner = lax.rem(my_inner + 4 - ij, 4)
            b = block_of(outer, inner)
            for part, dst in ((pl.ds(0, ROWS_IN), w_in), (pl.ds(ROWS_IN, ROWS_OUT), w_out)):
                copy = pltpu.make_async_copy(src.at[part, :], dst.at[b], wsem.at[n])
                copy.start()
                loads.append(copy)
                n += 1

    def flip(i, _):
        c = pl.multiple_of(i * 128, 128)
        xt[pl.ds(c, 128), :] = x_ref[0, :, pl.ds(c, 128)].T
        return 0

    lax.fori_loop(0, WIDTH // 128, flip, 0)
    for copy in loads:
        copy.wait()

    x = x_ref.at[0]
    dy = dy_ref.at[0]
    tile = 256
    sg_ref[...] = jnp.zeros_like(sg_ref)

    def forward(i, _):
        lo = pl.multiple_of(i * tile, tile)
        hi = pl.multiple_of(HID + i * tile, tile)
        wg = w_in[:, :, pl.ds(lo, tile)].reshape(WIDTH, tile)
        wu = w_in[:, :, pl.ds(hi, tile)].reshape(WIDTH, tile)
        wd = w_out[pl.ds(i * (tile // ROWS_OUT), tile // ROWS_OUT)].reshape(tile, WIDTH)
        gate_pre = dot(x[...], wg, NN)
        up_pre = dot(x[...], wu, NN)
        raw = dot(dy[...], wd, NT)
        prob = gate_ref[0, :, 0:1]
        s = jax.nn.sigmoid(gate_pre)
        silu = gate_pre * s
        activation = silu * up_pre
        act_grad = prob * raw
        d_gate = act_grad * up_pre * s * (1.0 + gate_pre * (1.0 - s))
        pre[:, pl.ds(lo, tile)] = d_gate.astype(BF16)
        pre[:, pl.ds(hi, tile)] = (act_grad * silu).astype(BF16)
        act[:, pl.ds(lo, tile)] = (prob * activation).astype(BF16)
        total = jnp.sum(activation * raw, axis=1, keepdims=True)
        sg_ref[...] += jnp.broadcast_to(total, sg_ref.shape)
        return 0

    lax.fori_loop(0, HID // tile, forward, 0)

    def flip_act(i, _):
        c = pl.multiple_of(i * 128, 128)
        at[pl.ds(c, 128), :] = act[:, pl.ds(c, 128)].T
        return 0

    lax.fori_loop(0, HID // 128, flip_act, 0)

    def backward(i, _):
        lo = pl.multiple_of(i * tile, tile)
        g_in = dot(xt[...], pre[:, pl.ds(lo, tile)], NN).astype(BF16)
        g_out = dot(at[...], dy[:, pl.ds(lo, tile)], NN).astype(BF16)
        for outer in range(4):
            for inner in range(4):
                b = block_of(outer, inner)
                oj = lax.rem(outer + 4 - my_outer, 4)
                ij = lax.rem(inner + 4 - my_inner, 4)
                grads[oj, ij, 0:ROWS_IN, pl.ds(lo, tile)] = g_in[b * ROWS_IN : (b + 1) * ROWS_IN]
                grads[oj, ij, ROWS_IN:ROWS, pl.ds(lo, tile)] = g_out[
                    b * ROWS_OUT : (b + 1) * ROWS_OUT
                ]
        return 0

    lax.fori_loop(0, WIDTH // tile, backward, 0)
    stores = [
        pltpu.make_async_copy(grads.at[2, pl.ds(0, 2)], g_far_a, gsem.at[0]),
        pltpu.make_async_copy(grads.at[2, pl.ds(2, 2)], g_far_b, gsem.at[1]),
        pltpu.make_async_copy(grads.at[1], g_up, gsem.at[2]),
        pltpu.make_async_copy(grads.at[3], g_dn, gsem.at[3]),
        pltpu.make_async_copy(grads.at[0], g_own, gsem.at[4]),
    ]
    for copy in stores:
        copy.start()

    def input_grad(i, _):
        b = i * (tile // ROWS_IN)
        w = w_in[pl.ds(b, tile // ROWS_IN)].reshape(tile, WIDTH)
        lo = pl.multiple_of(i * tile, tile)
        dx_ref[:, pl.ds(lo, tile)] = dot(pre[...], w, NT).astype(BF16)
        return 0

    lax.fori_loop(0, WIDTH // tile, input_grad, 0)
    for copy in stores:
        copy.wait()


def expert(e, inner_first, place, x, dy, gate, pieces):
    any_spec = pl.BlockSpec(memory_space=pl.ANY)
    return pl.pallas_call(
        functools.partial(expert_kernel, inner_first),
        name="expert",
        grid_spec=pltpu.PrefetchScalarGridSpec(
            num_scalar_prefetch=1,
            grid=(1,),
            in_specs=[
                pl.BlockSpec((1, SLOTS, WIDTH), lambda i, f: (e, 0, 0)),
                pl.BlockSpec((1, SLOTS, WIDTH), lambda i, f: (e, 0, 0)),
                pl.BlockSpec((1, SLOTS, TOK), lambda i, f: (e, 0, 0)),
            ]
            + [any_spec] * 5,
            out_specs=[any_spec] * 5
            + [
                pl.BlockSpec((SLOTS, WIDTH), lambda i, f: (0, 0)),
                pl.BlockSpec((SLOTS, TOK), lambda i, f: (0, 0)),
            ],
            scratch_shapes=[
                pltpu.VMEM((16, ROWS_IN, WIDTH), BF16),
                pltpu.VMEM((16, ROWS_OUT, WIDTH), BF16),
                pltpu.VMEM((SLOTS, WIDTH), BF16),
                pltpu.VMEM((SLOTS, HID), BF16),
                pltpu.VMEM((WIDTH, SLOTS), BF16),
                pltpu.VMEM((HID, SLOTS), BF16),
                pltpu.VMEM((4, 4, ROWS, WIDTH), BF16),
                pltpu.SemaphoreType.DMA((32,)),
                pltpu.SemaphoreType.DMA((5,)),
            ],
        ),
        out_shape=[
            jax.ShapeDtypeStruct((2, ROWS, WIDTH), BF16),
            jax.ShapeDtypeStruct((2, ROWS, WIDTH), BF16),
            jax.ShapeDtypeStruct((4, ROWS, WIDTH), BF16),
            jax.ShapeDtypeStruct((4, ROWS, WIDTH), BF16),
            jax.ShapeDtypeStruct((4, ROWS, WIDTH), BF16),
            jax.ShapeDtypeStruct((SLOTS, WIDTH), BF16),
            jax.ShapeDtypeStruct((SLOTS, TOK), F32),
        ],
        compiler_params=pltpu.CompilerParams(vmem_limit_bytes=VMEM_LIMIT),
        cost_estimate=pl.CostEstimate(
            flops=2 * 640 * 1024 * 4096, bytes_accessed=12_000_000, transcendentals=640 * 512
        ),
    )(place, x, dy, gate, *pieces)


def combine_kernel(first_ref, meta_ref, sel_ref, dx0_ref, dx1_ref, sg0_ref, sg1_ref, out_ref):
    first = first_ref[0]
    sel = sel_ref[0]
    rows = jnp.concatenate([dx0_ref[...], dx1_ref[...]], axis=0)
    back = dot(sel, rows, TN).astype(BF16)
    sums = jnp.concatenate([sg0_ref[:, 0:1], sg1_ref[:, 0:1]], axis=0)
    sums = sums.astype(BF16).astype(F32)
    spread = sel.astype(F32) * sums
    totals = [
        jnp.sum(spread[:PAIR], axis=0, keepdims=True),
        jnp.sum(spread[PAIR:], axis=0, keepdims=True),
    ]
    for c in range(2):
        out_ref[c, 0, 0:TOK] = back[c * TOK : (c + 1) * TOK]
        ids = meta_ref[c, :, 0:TOK].astype(F32)
        value = jnp.zeros((TOP, TOK), F32)
        for e in range(2):
            hit = ids == (first + e).astype(F32)
            value = value + jnp.where(hit, totals[e][:, c * TOK : (c + 1) * TOK], 0.0)
        out_ref[c, 0, TOK : TOK + TOP] = jnp.zeros((TOP, WIDTH), BF16)
        out_ref[c, 0, TOK : TOK + TOP, 0:TOK] = value.astype(BF16)


def combine(first, pay, sel, dx0, dx1, sg0, sg1):
    return pl.pallas_call(
        combine_kernel,
        name="combine",
        grid_spec=pltpu.PrefetchScalarGridSpec(
            num_scalar_prefetch=1,
            grid=(CHIPS,),
            in_specs=[
                pl.BlockSpec((2, TOP, 2 * TOK), lambda p, f: (p, 2 * TOK // TOP, 0)),
                pl.BlockSpec((1, 2 * PAIR, 2 * TOK), lambda p, f: (p, 0, 0)),
                pl.BlockSpec((PAIR, WIDTH), lambda p, f: (p, 0)),
                pl.BlockSpec((PAIR, WIDTH), lambda p, f: (p, 0)),
                pl.BlockSpec((PAIR, TOK), lambda p, f: (p, 0)),
                pl.BlockSpec((PAIR, TOK), lambda p, f: (p, 0)),
            ],
            out_specs=pl.BlockSpec((2, 1, TOK + TOP, WIDTH), lambda p, f: (0, p, 0, 0)),
        ),
        out_shape=jax.ShapeDtypeStruct((2, CHIPS, TOK + TOP, WIDTH), BF16),
        compiler_params=pltpu.CompilerParams(vmem_limit_bytes=VMEM_LIMIT),
        cost_estimate=pl.CostEstimate(
            flops=2 * 1280 * 256 * 1024, bytes_accessed=8_000_000, transcendentals=0
        ),
    )(first, pay, sel, dx0, dx1, sg0, sg1)


def gather_ring(block, axis):
    half = block.shape[0] // 2
    below = lax.ppermute(block, axis, UP)
    above = lax.ppermute(block, axis, DOWN)
    far_a = lax.ppermute(below[:half], axis, UP)
    far_b = lax.ppermute(above[half:], axis, DOWN)
    return block, below, above, far_a, far_b


def gather_weights(own, inner, outer):
    own, below, above, far_a, far_b = gather_ring(own, inner)
    far = jnp.concatenate([far_a, far_b], axis=0)
    row = jnp.stack([own, below, far, above], axis=0)
    return gather_ring(row, outer)


def add(a, b):
    return a.astype(F32) + b.astype(F32)


def reduce_ring(far_a, far_b, up, down, own, axis):
    half = far_a.shape[0]
    from_below = lax.ppermute(far_a, axis, UP)
    from_above = lax.ppermute(far_b, axis, DOWN)
    up = jnp.concatenate([add(up[:half], from_below).astype(BF16), up[half:]], axis=0)
    down = jnp.concatenate([down[:half], add(down[half:], from_above).astype(BF16)], axis=0)
    from_below = lax.ppermute(up, axis, UP)
    from_above = lax.ppermute(down, axis, DOWN)
    return add(own, from_below) + from_above.astype(F32)


def reduce_grads(pieces, outer, inner):
    total = reduce_ring(*pieces, outer)
    rounded = total.astype(BF16)
    half = ROWS // 2
    return reduce_ring(
        rounded[2, :half], rounded[2, half:], rounded[1], rounded[3], total[0], inner
    )


def body(tokens, cotangent, expert_ids, gate_probs, gate_up, down_proj):
    ix, iy = lax.axis_index("x"), lax.axis_index("y")
    first = (2 * (2 * lax.axis_index("z") + lax.axis_index("core"))).astype(jnp.int32)[None]
    meta = jnp.concatenate(
        [
            expert_ids.T.astype(BF16),
            gate_probs.T,
            jnp.zeros((TOP, WIDTH - 2 * TOK), BF16),
        ],
        axis=1,
    )
    pay = jnp.concatenate([tokens, cotangent, meta], axis=0)
    pay = lax.all_gather(pay, ("z", "core"), axis=0, tiled=False)
    own = jnp.concatenate([gate_up, down_proj], axis=1)
    pieces0 = gather_weights(own[0], "x", "y")
    pieces1 = gather_weights(own[1], "y", "x")
    place0 = jnp.stack([iy, ix]).astype(jnp.int32)
    place1 = jnp.stack([ix, iy]).astype(jnp.int32)

    x, dy, gate, sel = route(first, pay)
    *g0, dx0, sg0 = expert(0, False, place0, x, dy, gate, pieces0)
    *g1, dx1, sg1 = expert(1, True, place1, x, dy, gate, pieces1)
    total0 = reduce_grads(g0, "y", "x")
    total1 = reduce_grads(g1, "x", "y")

    part = combine(first, pay, sel, dx0, dx1, sg0, sg1)
    pair = lax.all_to_all(part, "core", split_axis=0, concat_axis=0, tiled=True)
    pair = add(pair[0], pair[1]).astype(BF16).reshape(CHIPS * (TOK + TOP), WIDTH)
    done = lax.psum_scatter(pair, "z", scatter_dimension=0, tiled=True)
    grad_tokens = done[:TOK]
    grad_gates = done[TOK:, :TOK].T
    grad_gate_up = jnp.stack([total0[:ROWS_IN], total1[:ROWS_IN]], axis=0)
    grad_down = jnp.stack([total0[ROWS_IN:], total1[ROWS_IN:]], axis=0)
    return grad_tokens, grad_gates, grad_gate_up, grad_down


def solution(mesh):
    grid = Mesh(mesh.devices.reshape(4, 4, 8, 2), ("y", "x", "z", "core"))
    rows = P(("y", "x", "z", "core"), None)
    held = P(("z", "core"), ("y", "x"), None)
    return jax.shard_map(
        body,
        mesh=grid,
        in_specs=(rows, rows, rows, rows, held, held),
        out_specs=(rows, rows, held, held),
        check_vma=False,
    )
```

```python
import functools

import jax
import jax.numpy as jnp
from jax import lax
from jax.experimental import pallas as pl
from jax.experimental.pallas import tpu as pltpu
from jax.sharding import Mesh
from jax.sharding import PartitionSpec as P

BF16 = jnp.bfloat16
F32 = jnp.float32
TOP = 8
CAP = 40
TOK = 128
WIDTH = 1024
HID = 512
ROWS_IN = 64
ROWS_OUT = 32
ROWS = ROWS_IN + ROWS_OUT
CHIPS = 8
PAIR = 2 * CAP
SLOTS = CHIPS * PAIR
MIB = 1024 * 1024

UP = [(i, (i + 1) % 4) for i in range(4)]
DOWN = [(i, (i - 1) % 4) for i in range(4)]


def dot(a, b, dims):
    return lax.dot_general(a, b, (dims, ((), ())), preferred_element_type=F32)


NN = ((1,), (0,))
NT = ((1,), (1,))
TN = ((0,), (0,))


def call(kernel, name, out_shape, *args, scalars=0, specs=None, out_specs=None, scratch=(), cost=None, limit=8, **more):
    vmem = pl.BlockSpec(memory_space=pltpu.VMEM)
    smem = pl.BlockSpec(memory_space=pltpu.SMEM)
    n = len(args) - scalars
    many = isinstance(out_shape, list)
    return pl.pallas_call(
        kernel,
        name=name,
        in_specs=[smem] * scalars + (specs or [vmem] * n),
        out_specs=out_specs or ([vmem] * len(out_shape) if many else vmem),
        out_shape=out_shape,
        scratch_shapes=list(scratch),
        compiler_params=pltpu.CompilerParams(vmem_limit_bytes=limit * MIB),
        cost_estimate=cost,
        **more,
    )(*args)


def cost(flops, nbytes):
    return pl.CostEstimate(flops=flops, bytes_accessed=nbytes, transcendentals=0)


def shape(*dims, dtype=BF16):
    return jax.ShapeDtypeStruct(dims, dtype)


ANY = pl.BlockSpec(memory_space=pl.ANY)
HBM = pl.BlockSpec(memory_space=pltpu.HBM)
VM = pl.BlockSpec(memory_space=pltpu.VMEM)


def pack_kernel(tok, cot, ids, probs, gu, dn, pay, own0, own1, buf, meta, wbuf, sem):
    halves = [
        pltpu.make_async_copy(tok, buf.at[0], sem.at[0]),
        pltpu.make_async_copy(cot, buf.at[1], sem.at[1]),
    ]
    weights = [
        pltpu.make_async_copy(gu, wbuf.at[:, pl.ds(0, ROWS_IN)], sem.at[2]),
        pltpu.make_async_copy(dn, wbuf.at[:, pl.ds(ROWS_IN, ROWS_OUT)], sem.at[3]),
    ]
    for copy in halves + weights:
        copy.start()
    meta[...] = jnp.zeros_like(meta)
    meta[:, 0:TOK] = ids[...].astype(F32).astype(BF16)
    meta[:, TOK : 2 * TOK] = probs[...]
    out = [pltpu.make_async_copy(meta, pay.at[pl.ds(2 * TOK, TOP)], sem.at[4])]
    out[0].start()
    for i in range(2):
        halves[i].wait()
        out.append(pltpu.make_async_copy(buf.at[i], pay.at[pl.ds(i * TOK, TOK)], sem.at[5 + i]))
        out[-1].start()
    for copy in weights:
        copy.wait()
    own0[...] = wbuf[0]
    own1[...] = wbuf[1]
    for copy in out:
        copy.wait()


def pack(tokens, cotangent, ids, probs, gate_up, down_proj):
    return call(
        pack_kernel,
        "pack",
        [shape(2 * TOK + TOP, WIDTH), shape(ROWS, WIDTH), shape(ROWS, WIDTH)],
        tokens,
        cotangent,
        ids,
        probs,
        gate_up,
        down_proj,
        specs=[HBM, HBM, VM, VM, HBM, HBM],
        out_specs=[HBM, VM, VM],
        limit=60,
        scratch=[
            pltpu.VMEM((2, TOK, WIDTH), BF16),
            pltpu.VMEM((TOP, WIDTH), BF16),
            pltpu.VMEM((2, ROWS, WIDTH), BF16),
            pltpu.SemaphoreType.DMA((7,)),
        ],
        cost=cost(0, 2_000_000),
    )


PIECES = ((4, ROWS, WIDTH),) * 3 + ((2, ROWS, WIDTH),) * 2
TILE = 256
START_AT = 2


def block_of(inner_first, outer, inner):
    return inner * 4 + outer if inner_first else outer * 4 + inner


def piece_of(refs, outer, inner):
    if outer != 2:
        return refs[(0, 1, None, 2)[outer]].at[inner]
    return refs[3].at[inner] if inner < 2 else refs[4].at[inner - 2]


def load_weights(inner_first, outer_pos, inner_pos, pieces, w_in, w_out, sem):
    copies = []
    for oj in range(4):
        for ij in range(4):
            src = piece_of(pieces, oj, ij)
            outer = lax.rem(outer_pos + 4 - oj, 4)
            inner = lax.rem(inner_pos + 4 - ij, 4)
            b = block_of(inner_first, outer, inner)
            n = 2 * (oj * 4 + ij)
            copies.append(pltpu.make_async_copy(src.at[pl.ds(0, ROWS_IN)], w_in.at[b], sem.at[n]))
            copies.append(
                pltpu.make_async_copy(
                    src.at[pl.ds(ROWS_IN, ROWS_OUT)], w_out.at[b], sem.at[n + 1]
                )
            )
    return copies


def route_pair(p, first, pay, x_ref, dy_ref, gate_ref, sel_ref, upper, slot):
    named, weights = [], []
    for e in range(2):
        expert = (first + e).astype(F32)
        for c in range(2):
            part = pay[2 * p + c, 2 * TOK : 2 * TOK + TOP, 0 : 2 * TOK]
            hit = jnp.where(part[:, :TOK].astype(F32) == expert, 1.0, 0.0)
            named.append(jnp.sum(hit, axis=0, keepdims=True))
            weights.append(jnp.sum(hit * part[:, TOK:].astype(F32), axis=0, keepdims=True))
    marks = jnp.concatenate(named + named, axis=0)
    ranks = dot(marks.astype(BF16), upper, NN)
    picks = []
    for e in range(2):
        halves = []
        for c in range(2):
            i = 2 * e + c
            at = jnp.where(marks[i : i + 1] > 0.5, ranks[i : i + 1] + float(CAP * c), -1.0)
            halves.append(jnp.where(slot == at, 1.0, 0.0))
        pick = jnp.concatenate(halves, axis=1)
        prob = jnp.concatenate([weights[2 * e], weights[2 * e + 1]], axis=1)
        column = jnp.sum(pick * prob, axis=1, keepdims=True)
        gate_ref[e, PAIR * p : PAIR * (p + 1)] = jnp.broadcast_to(column, (PAIR, TOK))
        picks.append(pick)
    sel = jnp.concatenate(picks, axis=0).astype(BF16)
    sel_ref[p] = sel
    rows = pl.ds(PAIR * p, PAIR)
    for lo, out in ((0, x_ref), (TOK, dy_ref)):
        both = jnp.concatenate([pay[2 * p, lo : lo + TOK], pay[2 * p + 1, lo : lo + TOK]], axis=0)
        routed = dot(sel, both, NN).astype(BF16)
        out[0, rows] = routed[:PAIR]
        out[1, rows] = routed[PAIR:]


def stores_of(held, grads, sem):
    own, up, down, far_a, far_b = grads
    return [
        pltpu.make_async_copy(held.at[2, pl.ds(0, 2)], far_a, sem.at[0]),
        pltpu.make_async_copy(held.at[2, pl.ds(2, 2)], far_b, sem.at[1]),
        pltpu.make_async_copy(held.at[1], up, sem.at[2]),
        pltpu.make_async_copy(held.at[3], down, sem.at[3]),
        pltpu.make_async_copy(held.at[0], own, sem.at[4]),
    ]


def expert_step(
    inner_first, outer_pos, inner_pos, x, dy, gate, w_in, w_out, held, grads, gsem, dx, sg,
    pre, act, xt, at, gin, gout,
):
    def flip(i, _):
        c = pl.multiple_of(i * 128, 128)
        xt[pl.ds(c, 128), :] = x[:, pl.ds(c, 128)].T
        return 0

    lax.fori_loop(0, WIDTH // 128, flip, 0, unroll=True)
    sg[...] = jnp.zeros_like(sg)

    def forward(i, _):
        lo = pl.multiple_of(i * TILE, TILE)
        hi = pl.multiple_of(HID + i * TILE, TILE)
        wg = w_in[:, :, pl.ds(lo, TILE)].reshape(WIDTH, TILE)
        wu = w_in[:, :, pl.ds(hi, TILE)].reshape(WIDTH, TILE)
        wd = w_out[pl.ds(i * (TILE // ROWS_OUT), TILE // ROWS_OUT)].reshape(TILE, WIDTH)
        gate_pre = dot(x[...], wg, NN)
        up_pre = dot(x[...], wu, NN)
        raw = dot(dy[...], wd, NT)
        prob = gate[:, 0:1]
        s = jax.nn.sigmoid(gate_pre)
        silu = gate_pre * s
        activation = silu * up_pre
        act_grad = prob * raw
        d_gate = act_grad * up_pre * s * (1.0 + gate_pre * (1.0 - s))
        pre[:, pl.ds(lo, TILE)] = d_gate.astype(BF16)
        pre[:, pl.ds(hi, TILE)] = (act_grad * silu).astype(BF16)
        act[:, pl.ds(lo, TILE)] = (prob * activation).astype(BF16)
        total = jnp.sum(activation * raw, axis=1, keepdims=True)
        sg[...] += jnp.broadcast_to(total, sg.shape)
        return 0

    lax.fori_loop(0, HID // TILE, forward, 0, unroll=True)

    def flip_act(i, _):
        c = pl.multiple_of(i * 128, 128)
        at[pl.ds(c, 128), :] = act[:, pl.ds(c, 128)].T
        return 0

    lax.fori_loop(0, HID // 128, flip_act, 0, unroll=True)

    def backward(i, _):
        cols = pl.ds(pl.multiple_of(i * TILE, TILE), TILE)
        gin[...] = dot(xt[...], pre[:, cols], NN).astype(BF16).reshape(gin.shape)
        gout[...] = dot(at[...], dy[:, cols], NN).astype(BF16).reshape(gout.shape)
        for oj in range(4):
            for ij in range(4):
                outer = lax.rem(outer_pos + oj, 4)
                inner = lax.rem(inner_pos + ij, 4)
                b = block_of(inner_first, outer, inner)
                held[oj, ij, 0:ROWS_IN, cols] = gin[b]
                held[oj, ij, ROWS_IN:ROWS, cols] = gout[b]
        return 0

    lax.fori_loop(0, WIDTH // TILE, backward, 0, unroll=True)
    for copy in stores_of(held, grads, gsem):
        copy.start()

    def input_grad(i, _):
        w = w_in[pl.ds(i * (TILE // ROWS_IN), TILE // ROWS_IN)].reshape(TILE, WIDTH)
        lo = pl.multiple_of(i * TILE, TILE)
        dx[:, pl.ds(lo, TILE)] = dot(pre[...], w, NT).astype(BF16)
        return 0

    lax.fori_loop(0, WIDTH // TILE, input_grad, 0, unroll=True)


def combine_pair(p, first, pay, sel_ref, dx, sg, part):
    sel = sel_ref[p]
    at = pl.ds(PAIR * p, PAIR)
    rows = jnp.concatenate([dx[0, at], dx[1, at]], axis=0)
    back = dot(sel, rows, TN).astype(BF16)
    sums = jnp.concatenate([sg[0, at, 0:1], sg[1, at, 0:1]], axis=0)
    sums = sums.astype(BF16).astype(F32)
    spread = sel.astype(F32) * sums
    totals = [
        jnp.sum(spread[:PAIR], axis=0, keepdims=True),
        jnp.sum(spread[PAIR:], axis=0, keepdims=True),
    ]
    for c in range(2):
        part[c, 0:TOK] = back[c * TOK : (c + 1) * TOK]
        ids = pay[2 * p + c, 2 * TOK : 2 * TOK + TOP, 0:TOK].astype(F32)
        value = jnp.zeros((TOP, TOK), F32)
        for e in range(2):
            hit = ids == (first + e).astype(F32)
            value = value + jnp.where(hit, totals[e][:, c * TOK : (c + 1) * TOK], 0.0)
        part[c, TOK : TOK + TOP] = jnp.zeros((TOP, WIDTH), BF16)
        part[c, TOK : TOK + TOP, 0:TOK] = value.astype(BF16)


def experts_kernel(where, pay_hbm, *refs):
    pieces = refs[0:5], refs[5:10]
    grads = refs[10:15], refs[15:20]
    keep, send = refs[20:22]
    pay, x, dy, gate, sel, dx, sg, w_in, w_out, pre, act, xt, at, gin, gout, part = refs[22:38]
    held, psem, wsem, gsem, csem = refs[38:]
    first, core, iy, ix = where[0], where[1], where[2], where[3]
    loads = [
        pltpu.make_async_copy(pay_hbm.at[pl.ds(2 * p, 2)], pay.at[pl.ds(2 * p, 2)], psem.at[p])
        for p in range(CHIPS)
    ]
    for copy in loads:
        copy.start()
    spots = (False, iy, ix), (True, ix, iy)
    weights = [
        load_weights(*spots[e], pieces[e], w_in.at[e], w_out.at[e], wsem.at[e]) for e in range(2)
    ]
    upper = (
        lax.broadcasted_iota(jnp.int32, (TOK, TOK), 0)
        < lax.broadcasted_iota(jnp.int32, (TOK, TOK), 1)
    ).astype(BF16)
    slot = lax.broadcasted_iota(jnp.int32, (PAIR, TOK), 0).astype(F32)
    for p in range(CHIPS):
        loads[p].wait()
        if p == START_AT:
            for copy in weights[0]:
                copy.start()
        route_pair(p, first, pay, x, dy, gate, sel, upper, slot)
    for e in range(2):
        for copy in weights[e]:
            copy.wait()
        if e == 0:
            for copy in weights[1]:
                copy.start()
        expert_step(
            *spots[e], x.at[e], dy.at[e], gate.at[e], w_in.at[e], w_out.at[e], held.at[e],
            grads[e], gsem.at[e], dx.at[e], sg.at[e], pre, act, xt, at, gin, gout,
        )

    outs = []
    for p in range(CHIPS):
        combine_pair(p, first, pay, sel, dx, sg, part.at[p])
        for i, (c, out) in enumerate(((core, keep), (1 - core, send))):
            copy = pltpu.make_async_copy(part.at[p, c], out.at[p], csem.at[2 * p + i])
            copy.start()
            outs.append(copy)
    for e in range(2):
        outs += stores_of(held.at[e], grads[e], gsem.at[e])
    for copy in outs:
        copy.wait()


def experts(where, pay, pieces0, pieces1):
    return call(
        experts_kernel,
        "experts",
        [shape(*dims) for dims in PIECES] * 2 + [shape(CHIPS, TOK + TOP, WIDTH)] * 2,
        where,
        pay,
        *pieces0,
        *pieces1,
        scalars=1,
        specs=[HBM] + [HBM] * 10,
        out_specs=[HBM] * 12,
        scratch=[
            pltpu.VMEM((2 * CHIPS, 2 * TOK + TOP, WIDTH), BF16),
            pltpu.VMEM((2, SLOTS, WIDTH), BF16),
            pltpu.VMEM((2, SLOTS, WIDTH), BF16),
            pltpu.VMEM((2, SLOTS, TOK), F32),
            pltpu.VMEM((CHIPS, 2 * PAIR, 2 * TOK), BF16),
            pltpu.VMEM((2, SLOTS, WIDTH), BF16),
            pltpu.VMEM((2, SLOTS, TOK), F32),
            pltpu.VMEM((2, 16, ROWS_IN, WIDTH), BF16),
            pltpu.VMEM((2, 16, ROWS_OUT, WIDTH), BF16),
            pltpu.VMEM((SLOTS, WIDTH), BF16),
            pltpu.VMEM((SLOTS, HID), BF16),
            pltpu.VMEM((WIDTH, SLOTS), BF16),
            pltpu.VMEM((HID, SLOTS), BF16),
            pltpu.VMEM((16, ROWS_IN, TILE), BF16),
            pltpu.VMEM((16, ROWS_OUT, TILE), BF16),
            pltpu.VMEM((CHIPS, 2, TOK + TOP, WIDTH), BF16),
            pltpu.VMEM((2, 4, 4, ROWS, WIDTH), BF16),
            pltpu.SemaphoreType.DMA((CHIPS,)),
            pltpu.SemaphoreType.DMA((2, 32)),
            pltpu.SemaphoreType.DMA((2, 5)),
            pltpu.SemaphoreType.DMA((2 * CHIPS,)),
        ],
        cost=cost(4 * 640 * 1024 * 4096, 20_000_000),
        limit=56,
    )


def add(a, b):
    return a.astype(F32) + b.astype(F32)


def fold_kernel(half, up_ref, below_ref, down_ref, above_ref, up_out, down_out):
    up_out[0:half] = add(up_ref[0:half], below_ref[...]).astype(BF16)
    up_out[half:] = up_ref[half:]
    down_out[0:half] = down_ref[0:half]
    down_out[half:] = add(down_ref[half:], above_ref[...]).astype(BF16)


def fold(up, below, down, above):
    return call(
        functools.partial(fold_kernel, below.shape[0]),
        "fold",
        [shape(*up.shape), shape(*up.shape)],
        up,
        below,
        down,
        above,
        cost=cost(0, 1024),
    )


def total_kernel(own, below, above, kept, far_a, far_b, up, down):
    half = ROWS // 2

    def total(i):
        return add(own[i], below[i]) + above[i].astype(F32)

    kept[...] = total(0)
    up[...] = total(1).astype(BF16)
    down[...] = total(3).astype(BF16)
    far = total(2).astype(BF16)
    far_a[...] = far[:half]
    far_b[...] = far[half:]


def total_of(own, below, above):
    half = ROWS // 2
    return call(
        total_kernel,
        "total",
        [
            shape(ROWS, WIDTH, dtype=F32),
            shape(half, WIDTH),
            shape(half, WIDTH),
            shape(ROWS, WIDTH),
            shape(ROWS, WIDTH),
        ],
        own,
        below,
        above,
        cost=cost(0, 1024),
    )


def finish_kernel(*refs):
    d_in, d_out = refs[6:]
    for e in range(2):
        kept, below, above = refs[3 * e : 3 * e + 3]
        total = kept[...] + below[...].astype(F32) + above[...].astype(F32)
        d_in[e] = total[:ROWS_IN]
        d_out[e] = total[ROWS_IN:]


def finish(*parts):
    return call(
        finish_kernel,
        "finish",
        [shape(2, ROWS_IN, WIDTH, dtype=F32), shape(2, ROWS_OUT, WIDTH, dtype=F32)],
        *parts,
        cost=cost(0, 1024),
    )


def join_kernel(a, b, out):
    out[...] = add(a[...], b[...]).astype(BF16)


def join(a, b):
    return call(join_kernel, "join", shape(*a.shape), a, b, cost=cost(0, 1024))


def gather_ring(block, axis):
    half = block.shape[0] // 2
    below = lax.ppermute(block, axis, UP)
    above = lax.ppermute(block, axis, DOWN)
    far_a = lax.ppermute(below[:half], axis, UP)
    far_b = lax.ppermute(above[half:], axis, DOWN)
    return block, below, above, far_a, far_b


def gather_weights(own, inner, outer):
    own, below, above, far_a, far_b = gather_ring(own, inner)
    far = jnp.concatenate([far_a, far_b], axis=0)
    row = jnp.stack([own, below, far, above], axis=0)
    return gather_ring(row, outer)


def swap(a, b, axis):
    return lax.ppermute(a, axis, UP), lax.ppermute(b, axis, DOWN)


def body(tokens, cotangent, expert_ids, gate_probs, gate_up, down_proj):
    ix = lax.axis_index("x").astype(jnp.int32)
    iy = lax.axis_index("y").astype(jnp.int32)
    core = lax.axis_index("core").astype(jnp.int32)
    first = (2 * (2 * lax.axis_index("z") + core)).astype(jnp.int32)
    where, ids = lax.optimization_barrier((jnp.stack([first, core, iy, ix]), expert_ids.T))
    pay, own0, own1 = pack(tokens, cotangent, ids, gate_probs.T, gate_up, down_proj)
    pay = lax.all_gather(pay, ("z", "core"), axis=0, tiled=False)
    pieces0 = gather_weights(own0, "x", "y")
    pieces1 = gather_weights(own1, "y", "x")

    out = experts(where, pay, pieces0, pieces1)
    mine0, up0, dn0, a0, b0 = out[:5]
    mine1, up1, dn1, a1, b1 = out[5:10]
    keep, send = out[10:]
    got = lax.ppermute(send, "core", [(0, 1), (1, 0)])
    from0 = swap(a0, b0, "y")
    from1 = swap(a1, b1, "x")
    up0, dn0 = fold(up0, from0[0], dn0, from0[1])
    up1, dn1 = fold(up1, from1[0], dn1, from1[1])

    pair = join(keep, got).reshape(CHIPS * (TOK + TOP), WIDTH)
    pair, up0, dn0, up1, dn1 = lax.optimization_barrier((pair, up0, dn0, up1, dn1))
    below0, above0 = swap(up0, dn0, "y")
    below1, above1 = swap(up1, dn1, "x")
    done = lax.psum_scatter(pair, "z", scatter_dimension=0, tiled=True)

    kept0, a0, b0, up0, dn0 = total_of(mine0, below0, above0)
    from0 = swap(a0, b0, "x")
    up0, dn0 = fold(up0, from0[0], dn0, from0[1])
    below0, above0 = swap(up0, dn0, "x")
    kept1, a1, b1, up1, dn1 = total_of(mine1, below1, above1)
    from1 = swap(a1, b1, "y")
    up1, dn1 = fold(up1, from1[0], dn1, from1[1])
    below1, above1 = swap(up1, dn1, "y")
    grad_tokens = done[:TOK]
    grad_gates = done[TOK:, :TOK].T
    grad_tokens, grad_gates, kept0, kept1 = lax.optimization_barrier(
        (grad_tokens, grad_gates, kept0, kept1)
    )
    grad_gate_up, grad_down = finish(kept0, below0, above0, kept1, below1, above1)
    return grad_tokens, grad_gates, grad_gate_up, grad_down


def solution(mesh):
    grid = Mesh(mesh.devices.reshape(4, 4, 8, 2), ("y", "x", "z", "core"))
    rows = P(("y", "x", "z", "core"), None)
    held = P(("z", "core"), ("y", "x"), None)
    return jax.shard_map(
        body,
        mesh=grid,
        in_specs=(rows, rows, rows, rows, held, held),
        out_specs=(rows, rows, held, held),
        check_vma=False,
    )
```

```python
import functools

import jax
import jax.numpy as jnp
from jax import lax
from jax.experimental import pallas as pl
from jax.experimental.pallas import tpu as pltpu
from jax.sharding import Mesh
from jax.sharding import PartitionSpec as P

BF16 = jnp.bfloat16
F32 = jnp.float32
TOP = 8
CAP = 40
TOK = 128
WIDTH = 1024
HID = 512
ROWS_IN = 64
ROWS_OUT = 32
ROWS = ROWS_IN + ROWS_OUT
CHIPS = 8
PAIR = 2 * CAP
SLOTS = CHIPS * PAIR
MIB = 1024 * 1024

UP = [(i, (i + 1) % 4) for i in range(4)]
DOWN = [(i, (i - 1) % 4) for i in range(4)]
ACROSS = [(i, (i + 2) % 4) for i in range(4)]


def dot(a, b, dims):
    return lax.dot_general(a, b, (dims, ((), ())), preferred_element_type=F32)


NN = ((1,), (0,))
NT = ((1,), (1,))
TN = ((0,), (0,))


def call(kernel, name, out_shape, *args, scalars=0, specs=None, out_specs=None, scratch=(), cost=None, limit=8, **more):
    vmem = pl.BlockSpec(memory_space=pltpu.VMEM)
    smem = pl.BlockSpec(memory_space=pltpu.SMEM)
    n = len(args) - scalars
    many = isinstance(out_shape, list)
    return pl.pallas_call(
        kernel,
        name=name,
        in_specs=[smem] * scalars + (specs or [vmem] * n),
        out_specs=out_specs or ([vmem] * len(out_shape) if many else vmem),
        out_shape=out_shape,
        scratch_shapes=list(scratch),
        compiler_params=pltpu.CompilerParams(vmem_limit_bytes=limit * MIB),
        cost_estimate=cost,
        **more,
    )(*args)


def cost(flops, nbytes):
    return pl.CostEstimate(flops=flops, bytes_accessed=nbytes, transcendentals=0)


def shape(*dims, dtype=BF16):
    return jax.ShapeDtypeStruct(dims, dtype)


ANY = pl.BlockSpec(memory_space=pl.ANY)
HBM = pl.BlockSpec(memory_space=pltpu.HBM)
VM = pl.BlockSpec(memory_space=pltpu.VMEM)


def pack_kernel(tok, cot, ids, probs, gu, dn, pay, own0, own1, buf, meta, wbuf, sem):
    halves = [
        pltpu.make_async_copy(tok, buf.at[0], sem.at[0]),
        pltpu.make_async_copy(cot, buf.at[1], sem.at[1]),
    ]
    weights = [
        pltpu.make_async_copy(gu, wbuf.at[:, pl.ds(0, ROWS_IN)], sem.at[2]),
        pltpu.make_async_copy(dn, wbuf.at[:, pl.ds(ROWS_IN, ROWS_OUT)], sem.at[3]),
    ]
    for copy in halves + weights:
        copy.start()
    meta[...] = jnp.zeros_like(meta)
    meta[:, 0:TOK] = ids[...].astype(F32).astype(BF16)
    meta[:, TOK : 2 * TOK] = probs[...]
    out = [pltpu.make_async_copy(meta, pay.at[pl.ds(2 * TOK, TOP)], sem.at[4])]
    out[0].start()
    for i in range(2):
        halves[i].wait()
        out.append(pltpu.make_async_copy(buf.at[i], pay.at[pl.ds(i * TOK, TOK)], sem.at[5 + i]))
        out[-1].start()
    for copy in weights:
        copy.wait()
    for i in range(4):
        own0[i] = wbuf[0]
        own1[i] = wbuf[1]
    for copy in out:
        copy.wait()


def pack(tokens, cotangent, ids, probs, gate_up, down_proj):
    return call(
        pack_kernel,
        "pack",
        [shape(2 * TOK + TOP, WIDTH), shape(4, ROWS, WIDTH), shape(4, ROWS, WIDTH)],
        tokens,
        cotangent,
        ids,
        probs,
        gate_up,
        down_proj,
        specs=[HBM, HBM, VM, VM, HBM, HBM],
        out_specs=[HBM, VM, VM],
        limit=60,
        scratch=[
            pltpu.VMEM((2, TOK, WIDTH), BF16),
            pltpu.VMEM((TOP, WIDTH), BF16),
            pltpu.VMEM((2, ROWS, WIDTH), BF16),
            pltpu.SemaphoreType.DMA((7,)),
        ],
        cost=cost(0, 2_000_000),
    )


PIECES = ((4, ROWS, WIDTH),) * 3 + ((2, ROWS, WIDTH),) * 2
TILE = 256
START_AT = 2


def load_weights(e, outer_pos, pieces, w_in, w_out, sem):
    own, below, above, far_a, far_b = pieces
    copies = []
    for offset, lo, src in ((0, 0, own), (1, 0, below), (3, 0, above), (2, 0, far_a), (2, 2, far_b)):
        outer = lax.rem(outer_pos + 4 - offset, 4)
        inner = pl.ds(lo, src.shape[0])
        for rows, dst in ((pl.ds(0, ROWS_IN), w_in), (pl.ds(ROWS_IN, ROWS_OUT), w_out)):
            at = dst.at[outer, inner] if e == 0 else dst.at[inner, outer]
            copies.append(pltpu.make_async_copy(src.at[:, rows], at, sem.at[len(copies)]))
    return copies


def route_pair(p, first, pay, x_ref, dy_ref, gate_ref, sel_ref, upper, slot):
    named, weights = [], []
    for e in range(2):
        expert = (first + e).astype(F32)
        for c in range(2):
            part = pay[2 * p + c, 2 * TOK : 2 * TOK + TOP, 0 : 2 * TOK]
            hit = jnp.where(part[:, :TOK].astype(F32) == expert, 1.0, 0.0)
            named.append(jnp.sum(hit, axis=0, keepdims=True))
            weights.append(jnp.sum(hit * part[:, TOK:].astype(F32), axis=0, keepdims=True))
    marks = jnp.concatenate(named + named, axis=0)
    ranks = dot(marks.astype(BF16), upper, NN)
    picks = []
    for e in range(2):
        halves = []
        for c in range(2):
            i = 2 * e + c
            at = jnp.where(marks[i : i + 1] > 0.5, ranks[i : i + 1] + float(CAP * c), -1.0)
            halves.append(jnp.where(slot == at, 1.0, 0.0))
        pick = jnp.concatenate(halves, axis=1)
        prob = jnp.concatenate([weights[2 * e], weights[2 * e + 1]], axis=1)
        column = jnp.sum(pick * prob, axis=1, keepdims=True)
        gate_ref[e, PAIR * p : PAIR * (p + 1)] = jnp.broadcast_to(column, (PAIR, TOK))
        picks.append(pick)
    sel = jnp.concatenate(picks, axis=0).astype(BF16)
    sel_ref[p] = sel
    rows = pl.ds(PAIR * p, PAIR)
    for lo, out in ((0, x_ref), (TOK, dy_ref)):
        both = jnp.concatenate([pay[2 * p, lo : lo + TOK], pay[2 * p + 1, lo : lo + TOK]], axis=0)
        routed = dot(sel, both, NN).astype(BF16)
        out[0, rows] = routed[:PAIR]
        out[1, rows] = routed[PAIR:]


def stores_of(held, grads, sem):
    own, up, down, far_a, far_b = grads
    return [
        pltpu.make_async_copy(held.at[2, pl.ds(0, 2)], far_a, sem.at[0]),
        pltpu.make_async_copy(held.at[2, pl.ds(2, 2)], far_b, sem.at[1]),
        pltpu.make_async_copy(held.at[1], up, sem.at[2]),
        pltpu.make_async_copy(held.at[3], down, sem.at[3]),
        pltpu.make_async_copy(held.at[0], own, sem.at[4]),
    ]


def expert_step(
    first, outer_pos, inner_pos, x, dy, gate, w_in, w_out, held, dx, sg,
    pre, act, xt, at, gin, gout,
):
    def flip(i, _):
        c = pl.multiple_of(i * 128, 128)
        xt[pl.ds(c, 128), :] = x[:, pl.ds(c, 128)].T
        return 0

    lax.fori_loop(0, WIDTH // 128, flip, 0, unroll=True)
    sg[...] = jnp.zeros_like(sg)

    def forward(i, _):
        lo = pl.multiple_of(i * TILE, TILE)
        hi = pl.multiple_of(HID + i * TILE, TILE)
        wg = w_in[:, :, :, pl.ds(lo, TILE)].reshape(WIDTH, TILE)
        wu = w_in[:, :, :, pl.ds(hi, TILE)].reshape(WIDTH, TILE)
        wd = w_out[pl.ds(2 * i, 2)].reshape(TILE, WIDTH)
        gate_pre = dot(x[...], wg, NN)
        up_pre = dot(x[...], wu, NN)
        raw = dot(dy[...], wd, NT)
        prob = gate[:, 0:1]
        s = jax.nn.sigmoid(gate_pre)
        silu = gate_pre * s
        activation = silu * up_pre
        act_grad = prob * raw
        d_gate = act_grad * up_pre * s * (1.0 + gate_pre * (1.0 - s))
        pre[:, pl.ds(lo, TILE)] = d_gate.astype(BF16)
        pre[:, pl.ds(hi, TILE)] = (act_grad * silu).astype(BF16)
        act[:, pl.ds(lo, TILE)] = (prob * activation).astype(BF16)
        total = jnp.sum(activation * raw, axis=1, keepdims=True)
        sg[...] += jnp.broadcast_to(total, sg.shape)
        return 0

    lax.fori_loop(0, HID // TILE, forward, 0, unroll=True)

    def flip_act(i, _):
        c = pl.multiple_of(i * 128, 128)
        at[pl.ds(c, 128), :] = act[:, pl.ds(c, 128)].T
        return 0

    lax.fori_loop(0, HID // 128, flip_act, 0, unroll=True)

    def backward(i, _):
        cols = pl.ds(pl.multiple_of(i * TILE, TILE), TILE)
        gin[...] = dot(xt[...], pre[:, cols], NN).astype(BF16).reshape(gin.shape)
        gout[...] = dot(at[...], dy[:, cols], NN).astype(BF16).reshape(gout.shape)
        for oj in range(4):
            for ij in range(4):
                outer = lax.rem(outer_pos + oj, 4)
                inner = lax.rem(inner_pos + ij, 4)
                b = jnp.where(first, outer * 4 + inner, inner * 4 + outer)
                held[oj, ij, 0:ROWS_IN, cols] = gin[b]
                held[oj, ij, ROWS_IN:ROWS, cols] = gout[b]
        return 0

    lax.fori_loop(0, WIDTH // TILE, backward, 0, unroll=True)

    def input_grad(i, _):
        w = w_in[i].reshape(TILE, WIDTH)
        lo = pl.multiple_of(i * TILE, TILE)
        dx[:, pl.ds(lo, TILE)] = dot(pre[...], w, NT).astype(BF16)
        return 0

    lax.fori_loop(0, WIDTH // TILE, input_grad, 0, unroll=True)


def combine_pair(p, first, pay, sel_ref, dx, sg, part):
    sel = sel_ref[p]
    at = pl.ds(PAIR * p, PAIR)
    rows = jnp.concatenate([dx[0, at], dx[1, at]], axis=0)
    back = dot(sel, rows, TN).astype(BF16)
    sums = jnp.concatenate([sg[0, at, 0:1], sg[1, at, 0:1]], axis=0)
    sums = sums.astype(BF16).astype(F32)
    spread = sel.astype(F32) * sums
    totals = [
        jnp.sum(spread[:PAIR], axis=0, keepdims=True),
        jnp.sum(spread[PAIR:], axis=0, keepdims=True),
    ]
    for c in range(2):
        part[c, 0:TOK] = back[c * TOK : (c + 1) * TOK]
        ids = pay[2 * p + c, 2 * TOK : 2 * TOK + TOP, 0:TOK].astype(F32)
        value = jnp.zeros((TOP, TOK), F32)
        for e in range(2):
            hit = ids == (first + e).astype(F32)
            value = value + jnp.where(hit, totals[e][:, c * TOK : (c + 1) * TOK], 0.0)
        part[c, TOK : TOK + TOP] = jnp.zeros((TOP, WIDTH), BF16)
        part[c, TOK : TOK + TOP, 0:TOK] = value.astype(BF16)


def experts_kernel(where, pay_hbm, *refs):
    pieces = refs[0:5], refs[5:10]
    grads = refs[10:15], refs[15:20]
    keep, send = refs[20:22]
    pay, x, dy, gate, sel, dx, sg, w_in, w_out, pre, act, xt, at, gin, gout, part = refs[22:38]
    held, psem, wsem, gsem, csem = refs[38:]
    first, core, iy, ix = where[0], where[1], where[2], where[3]
    loads = [
        pltpu.make_async_copy(pay_hbm.at[pl.ds(2 * p, 2)], pay.at[pl.ds(2 * p, 2)], psem.at[p])
        for p in range(CHIPS)
    ]
    for copy in loads:
        copy.start()
    weights = [
        load_weights(e, (iy, ix)[e], pieces[e], w_in.at[e], w_out.at[e], wsem.at[e])
        for e in range(2)
    ]
    upper = (
        lax.broadcasted_iota(jnp.int32, (TOK, TOK), 0)
        < lax.broadcasted_iota(jnp.int32, (TOK, TOK), 1)
    ).astype(BF16)
    slot = lax.broadcasted_iota(jnp.int32, (PAIR, TOK), 0).astype(F32)
    for p in range(CHIPS):
        loads[p].wait()
        if p == START_AT:
            for copy in weights[0]:
                copy.start()
        route_pair(p, first, pay, x, dy, gate, sel, upper, slot)

    def one(e, _):
        for n in range(10):
            src = pieces[0][(0, 0, 0, 3, 3)[n // 2]]
            rows, dst = ((pl.ds(0, ROWS_IN), w_in), (pl.ds(ROWS_IN, ROWS_OUT), w_out))[n % 2]
            inner = pl.ds(0, src.shape[0])
            pltpu.make_async_copy(src.at[:, rows], dst.at[e, 0, inner], wsem.at[e, n]).wait()

        @pl.when(e == 0)
        def _():
            for copy in weights[1]:
                copy.start()

        outer_pos = jnp.where(e == 0, iy, ix)
        inner_pos = jnp.where(e == 0, ix, iy)
        expert_step(
            e == 0, outer_pos, inner_pos, x.at[e], dy.at[e], gate.at[e], w_in.at[e], w_out.at[e],
            held.at[e], dx.at[e], sg.at[e], pre, act, xt, at, gin, gout,
        )
        for i in range(2):

            @pl.when(e == i)
            def _():
                for copy in stores_of(held.at[i], grads[i], gsem.at[i]):
                    copy.start()

        return 0

    lax.fori_loop(0, 2, one, 0)
    outs = []
    for p in range(CHIPS):
        combine_pair(p, first, pay, sel, dx, sg, part.at[p])
        for i, (c, out) in enumerate(((core, keep), (1 - core, send))):
            copy = pltpu.make_async_copy(part.at[p, c], out.at[p], csem.at[2 * p + i])
            copy.start()
            outs.append(copy)
    for e in range(2):
        outs += stores_of(held.at[e], grads[e], gsem.at[e])
    for copy in outs:
        copy.wait()


def experts(where, pay, pieces0, pieces1):
    near = pltpu.VMEM((4, ROWS, WIDTH), BF16)
    return call(
        experts_kernel,
        "experts",
        [shape(4, ROWS, WIDTH), near, near, *[shape(2, ROWS, WIDTH)] * 2] * 2
        + [pltpu.VMEM((CHIPS, TOK + TOP, WIDTH), BF16), shape(CHIPS, TOK + TOP, WIDTH)],
        where,
        pay,
        *pieces0,
        *pieces1,
        scalars=1,
        specs=[HBM] + [HBM] * 10,
        out_specs=[HBM, VM, VM, HBM, HBM] * 2 + [VM, HBM],
        scratch=[
            pltpu.VMEM((2 * CHIPS, 2 * TOK + TOP, WIDTH), BF16),
            pltpu.VMEM((2, SLOTS, WIDTH), BF16),
            pltpu.VMEM((2, SLOTS, WIDTH), BF16),
            pltpu.VMEM((2, SLOTS, TOK), F32),
            pltpu.VMEM((CHIPS, 2 * PAIR, 2 * TOK), BF16),
            pltpu.VMEM((2, SLOTS, WIDTH), BF16),
            pltpu.VMEM((2, SLOTS, TOK), F32),
            pltpu.VMEM((2, 4, 4, ROWS_IN, WIDTH), BF16),
            pltpu.VMEM((2, 4, 4, ROWS_OUT, WIDTH), BF16),
            pltpu.VMEM((SLOTS, WIDTH), BF16),
            pltpu.VMEM((SLOTS, HID), BF16),
            pltpu.VMEM((WIDTH, SLOTS), BF16),
            pltpu.VMEM((HID, SLOTS), BF16),
            pltpu.VMEM((16, ROWS_IN, TILE), BF16),
            pltpu.VMEM((16, ROWS_OUT, TILE), BF16),
            pltpu.VMEM((CHIPS, 2, TOK + TOP, WIDTH), BF16),
            pltpu.VMEM((2, 4, 4, ROWS, WIDTH), BF16),
            pltpu.SemaphoreType.DMA((CHIPS,)),
            pltpu.SemaphoreType.DMA((2, 10)),
            pltpu.SemaphoreType.DMA((2, 5)),
            pltpu.SemaphoreType.DMA((2 * CHIPS,)),
        ],
        cost=cost(4 * 640 * 1024 * 4096, 20_000_000),
        limit=50,
    )


def add(a, b):
    return a.astype(F32) + b.astype(F32)


def fold_kernel(*refs):
    blocks, arrived, (keep, got) = refs[0:4], refs[4:8], refs[8:10]
    outs, pair = refs[10:14], refs[14]
    block_buf, pair_buf, sem = refs[15:]
    pair_buf[...] = add(keep[...], got[...]).astype(BF16)
    stores = [pltpu.make_async_copy(pair_buf, pair, sem.at[4])]
    stores[0].start()
    for i in range(4):
        lo = 2 * (i % 2)
        block_buf[i, lo : lo + 2] = add(blocks[i][lo : lo + 2], arrived[i][...]).astype(BF16)
        block_buf[i, 2 - lo : 4 - lo] = blocks[i][2 - lo : 4 - lo]
        stores.append(pltpu.make_async_copy(block_buf.at[i], outs[i], sem.at[i]))
        stores[-1].start()
    for copy in stores:
        copy.wait()


def fold(*parts):
    return call(
        fold_kernel,
        "fold",
        [shape(4, ROWS, WIDTH)] * 4 + [shape(CHIPS, TOK + TOP, WIDTH)],
        *parts,
        out_specs=[HBM] * 5,
        scratch=[
            pltpu.VMEM((4, 4, ROWS, WIDTH), BF16),
            pltpu.VMEM((CHIPS, TOK + TOP, WIDTH), BF16),
            pltpu.SemaphoreType.DMA((5,)),
        ],
        cost=cost(0, 1024),
        limit=16,
    )


def total_kernel(*refs):
    for e in range(2):
        own, below, above = refs[3 * e : 3 * e + 3]
        outs = refs[6 + 4 * e : 10 + 4 * e]
        for i in range(4):
            value = add(own[i], below[i]) + above[i].astype(F32)
            outs[i][...] = value if i == 0 else value.astype(BF16)


def totals_of(*parts):
    outs = [shape(ROWS, WIDTH, dtype=F32)] + [shape(ROWS, WIDTH)] * 3
    return call(total_kernel, "total", outs * 2, *parts, cost=cost(0, 1024))


def finish_kernel(*refs):
    done = refs[8]
    d_tok, d_gate, d_in, d_out = refs[9:]
    for e in range(2):
        kept, a, b, c = refs[4 * e : 4 * e + 4]
        total = kept[...] + a[...].astype(F32) + b[...].astype(F32) + c[...].astype(F32)
        d_in[e] = total[:ROWS_IN]
        d_out[e] = total[ROWS_IN:]
    d_tok[...] = done[:TOK]
    d_gate[...] = done[TOK:, :TOK]


def finish(*parts):
    return call(
        finish_kernel,
        "finish",
        [
            shape(TOK, WIDTH),
            shape(TOP, TOK),
            shape(2, ROWS_IN, WIDTH, dtype=F32),
            shape(2, ROWS_OUT, WIDTH, dtype=F32),
        ],
        *parts,
        cost=cost(0, 1024),
    )


def gather_ring(block, axis):
    half = block.shape[0] // 2
    below = lax.ppermute(block, axis, UP)
    above = lax.ppermute(block, axis, DOWN)
    far_a = lax.ppermute(below[:half], axis, UP)
    far_b = lax.ppermute(above[half:], axis, DOWN)
    return block, below, above, far_a, far_b


def gather_weights(own, inner, outer):
    return gather_ring(lax.all_to_all(own, inner, split_axis=0, concat_axis=0, tiled=True), outer)


def swap(a, b, axis):
    return lax.ppermute(a, axis, UP), lax.ppermute(b, axis, DOWN)


def spread(parts, axis):
    kept, up, far, down = parts
    up, down = swap(up, down, axis)
    return kept, up, lax.ppermute(far, axis, ACROSS), down


def body(tokens, cotangent, expert_ids, gate_probs, gate_up, down_proj):
    ix = lax.axis_index("x").astype(jnp.int32)
    iy = lax.axis_index("y").astype(jnp.int32)
    core = lax.axis_index("core").astype(jnp.int32)
    first = (2 * (2 * lax.axis_index("z") + core)).astype(jnp.int32)
    where, ids = lax.optimization_barrier((jnp.stack([first, core, iy, ix]), expert_ids.T))
    pay, own0, own1 = pack(tokens, cotangent, ids, gate_probs.T, gate_up, down_proj)
    pay = lax.all_gather(pay, ("z", "core"), axis=0, tiled=False)
    pieces0 = gather_weights(own0, "x", "y")
    pieces1 = gather_weights(own1, "y", "x")

    out = experts(where, pay, pieces0, pieces1)
    mine0, up0, dn0, a0, b0 = out[:5]
    mine1, up1, dn1, a1, b1 = out[5:10]
    keep, send = out[10:]
    got = lax.ppermute(send, "core", [(0, 1), (1, 0)])
    below0, above0 = swap(a0, b0, "y")
    below1, above1 = swap(a1, b1, "x")
    up0, dn0, up1, dn1, pair = fold(
        up0, dn0, up1, dn1, below0, above0, below1, above1, keep, got
    )
    below0, above0 = swap(up0, dn0, "y")
    below1, above1 = swap(up1, dn1, "x")
    done = lax.psum_scatter(
        pair.reshape(CHIPS * (TOK + TOP), WIDTH), "z", scatter_dimension=0, tiled=True
    )
    out = totals_of(mine0, below0, above0, mine1, below1, above1)
    grad_tokens, grad_gates, grad_gate_up, grad_down = finish(
        *spread(out[:4], "x"), *spread(out[4:], "y"), done
    )
    return grad_tokens, grad_gates.T, grad_gate_up, grad_down


def solution(mesh):
    grid = Mesh(mesh.devices.reshape(4, 4, 8, 2), ("y", "x", "z", "core"))
    rows = P(("y", "x", "z", "core"), None)
    held = P(("z", "core"), ("y", "x"), None)
    return jax.shard_map(
        body,
        mesh=grid,
        in_specs=(rows, rows, rows, rows, held, held),
        out_specs=(rows, rows, held, held),
        check_vma=False,
    )
```

```python
import functools

import jax
import jax.numpy as jnp
from jax import lax
from jax.experimental import pallas as pl
from jax.experimental.pallas import tpu as pltpu
from jax.sharding import Mesh
from jax.sharding import PartitionSpec as P

BF16 = jnp.bfloat16
F32 = jnp.float32
TOP = 8
CAP = 40
TOK = 128
WIDTH = 1024
HID = 512
ROWS_IN = 64
ROWS_OUT = 32
ROWS = ROWS_IN + ROWS_OUT
CHIPS = 8
PAIR = 2 * CAP
SLOTS = CHIPS * PAIR
MIB = 1024 * 1024

UP = [(i, (i + 1) % 4) for i in range(4)]
DOWN = [(i, (i - 1) % 4) for i in range(4)]
ACROSS = [(i, (i + 2) % 4) for i in range(4)]


def dot(a, b, dims):
    return lax.dot_general(a, b, (dims, ((), ())), preferred_element_type=F32)


NN = ((1,), (0,))
NT = ((1,), (1,))
TN = ((0,), (0,))


def call(kernel, name, out_shape, *args, scalars=0, specs=None, out_specs=None, scratch=(), cost=None, limit=8, **more):
    vmem = pl.BlockSpec(memory_space=pltpu.VMEM)
    smem = pl.BlockSpec(memory_space=pltpu.SMEM)
    n = len(args) - scalars
    many = isinstance(out_shape, list)
    return pl.pallas_call(
        kernel,
        name=name,
        in_specs=[smem] * scalars + (specs or [vmem] * n),
        out_specs=out_specs or ([vmem] * len(out_shape) if many else vmem),
        out_shape=out_shape,
        scratch_shapes=list(scratch),
        compiler_params=pltpu.CompilerParams(vmem_limit_bytes=limit * MIB),
        cost_estimate=cost,
        **more,
    )(*args)


def cost(flops, nbytes):
    return pl.CostEstimate(flops=flops, bytes_accessed=nbytes, transcendentals=0)


def shape(*dims, dtype=BF16):
    return jax.ShapeDtypeStruct(dims, dtype)


ANY = pl.BlockSpec(memory_space=pl.ANY)
HBM = pl.BlockSpec(memory_space=pltpu.HBM)
VM = pl.BlockSpec(memory_space=pltpu.VMEM)


def pack_kernel(tok, cot, ids, probs, pay, buf, meta, sem):
    halves = [
        pltpu.make_async_copy(tok, buf.at[0], sem.at[0]),
        pltpu.make_async_copy(cot, buf.at[1], sem.at[1]),
    ]
    for copy in halves:
        copy.start()
    meta[...] = jnp.zeros_like(meta)
    meta[:, 0:TOK] = ids[...].astype(F32).astype(BF16)
    meta[:, TOK : 2 * TOK] = probs[...]
    out = [pltpu.make_async_copy(meta, pay.at[pl.ds(2 * TOK, TOP)], sem.at[2])]
    out[0].start()
    for i in range(2):
        halves[i].wait()
        out.append(pltpu.make_async_copy(buf.at[i], pay.at[pl.ds(i * TOK, TOK)], sem.at[3 + i]))
        out[-1].start()
    for copy in out:
        copy.wait()


def pack(tokens, cotangent, ids, probs):
    return call(
        pack_kernel,
        "pack",
        shape(2 * TOK + TOP, WIDTH),
        tokens,
        cotangent,
        ids,
        probs,
        specs=[HBM, HBM, VM, VM],
        out_specs=HBM,
        limit=60,
        scratch=[
            pltpu.VMEM((2, TOK, WIDTH), BF16),
            pltpu.VMEM((TOP, WIDTH), BF16),
            pltpu.SemaphoreType.DMA((5,)),
        ],
        cost=cost(0, 2_000_000),
    )


def rows_kernel(gu, dn, own0, own1):
    for e, own in enumerate((own0, own1)):
        own[0:ROWS_IN] = gu[e]
        own[ROWS_IN:ROWS] = dn[e]


def own_rows(gate_up, down_proj):
    return call(
        rows_kernel, "own_rows", [shape(ROWS, WIDTH)] * 2, gate_up, down_proj, cost=cost(0, 800_000)
    )


def place_kernel(index, me_ref, own, below, across, above, out):
    for j, block in enumerate((own, below, across, above)):
        out[lax.rem(me_ref[index] + 4 - j, 4)] = block[...]


def place(index, where, own, below, across, above):
    return call(
        functools.partial(place_kernel, index),
        "place",
        shape(4, ROWS, WIDTH),
        where,
        own,
        below,
        across,
        above,
        scalars=1,
        cost=cost(0, 1_600_000),
    )


TILE = 256
START_AT = 2


def load_weights(e, outer_pos, pieces, w_in, w_out, sem):
    own, below, above, far_a, far_b = pieces
    copies = []
    for offset, lo, src in ((0, 0, own), (1, 0, below), (3, 0, above), (2, 0, far_a), (2, 2, far_b)):
        outer = lax.rem(outer_pos + 4 - offset, 4)
        inner = pl.ds(lo, src.shape[0])
        for rows, dst in ((pl.ds(0, ROWS_IN), w_in), (pl.ds(ROWS_IN, ROWS_OUT), w_out)):
            at = dst.at[outer, inner] if e == 0 else dst.at[inner, outer]
            copies.append(pltpu.make_async_copy(src.at[:, rows], at, sem.at[len(copies)]))
    return copies


def route_pair(p, first, pay, x_ref, dy_ref, gate_ref, sel_ref, upper, slot):
    named, weights = [], []
    for e in range(2):
        expert = (first + e).astype(F32)
        for c in range(2):
            part = pay[2 * p + c, 2 * TOK : 2 * TOK + TOP, 0 : 2 * TOK]
            hit = jnp.where(part[:, :TOK].astype(F32) == expert, 1.0, 0.0)
            named.append(jnp.sum(hit, axis=0, keepdims=True))
            weights.append(jnp.sum(hit * part[:, TOK:].astype(F32), axis=0, keepdims=True))
    marks = jnp.concatenate(named + named, axis=0)
    ranks = dot(marks.astype(BF16), upper, NN)
    picks = []
    for e in range(2):
        halves = []
        for c in range(2):
            i = 2 * e + c
            at = jnp.where(marks[i : i + 1] > 0.5, ranks[i : i + 1] + float(CAP * c), -1.0)
            halves.append(jnp.where(slot == at, 1.0, 0.0))
        pick = jnp.concatenate(halves, axis=1)
        prob = jnp.concatenate([weights[2 * e], weights[2 * e + 1]], axis=1)
        column = jnp.sum(pick * prob, axis=1, keepdims=True)
        gate_ref[e, pl.ds(pl.multiple_of(PAIR * p, PAIR), PAIR)] = jnp.broadcast_to(column, (PAIR, TOK))
        picks.append(pick)
    sel = jnp.concatenate(picks, axis=0).astype(BF16)
    sel_ref[p] = sel
    rows = pl.ds(pl.multiple_of(PAIR * p, PAIR), PAIR)
    for lo, out in ((0, x_ref), (TOK, dy_ref)):
        both = jnp.concatenate([pay[2 * p, lo : lo + TOK], pay[2 * p + 1, lo : lo + TOK]], axis=0)
        routed = dot(sel, both, NN).astype(BF16)
        out[0, rows] = routed[:PAIR]
        out[1, rows] = routed[PAIR:]


def stores_of(held, grads, sem):
    own, up, down, far_a, far_b = grads
    return [
        pltpu.make_async_copy(held.at[2, pl.ds(0, 2)], far_a, sem.at[0]),
        pltpu.make_async_copy(held.at[2, pl.ds(2, 2)], far_b, sem.at[1]),
        pltpu.make_async_copy(held.at[1], up, sem.at[2]),
        pltpu.make_async_copy(held.at[3], down, sem.at[3]),
        pltpu.make_async_copy(held.at[0], own, sem.at[4]),
    ]


def expert_step(
    first, outer_pos, inner_pos, x, dy, gate, w_in, w_out, held, dx, sg,
    pre, act, xt, at, gin, gout,
):
    def flip(i, _):
        c = pl.multiple_of(i * 128, 128)
        xt[pl.ds(c, 128), :] = x[:, pl.ds(c, 128)].T
        return 0

    lax.fori_loop(0, WIDTH // 128, flip, 0, unroll=True)
    sg[...] = jnp.zeros_like(sg)

    def forward(i, _):
        lo = pl.multiple_of(i * TILE, TILE)
        hi = pl.multiple_of(HID + i * TILE, TILE)
        wg = w_in[:, :, :, pl.ds(lo, TILE)].reshape(WIDTH, TILE)
        wu = w_in[:, :, :, pl.ds(hi, TILE)].reshape(WIDTH, TILE)
        wd = w_out[pl.ds(2 * i, 2)].reshape(TILE, WIDTH)
        gate_pre = dot(x[...], wg, NN)
        up_pre = dot(x[...], wu, NN)
        raw = dot(dy[...], wd, NT)
        prob = gate[:, 0:1]
        s = jax.nn.sigmoid(gate_pre)
        silu = gate_pre * s
        activation = silu * up_pre
        act_grad = prob * raw
        d_gate = act_grad * up_pre * s * (1.0 + gate_pre * (1.0 - s))
        pre[:, pl.ds(lo, TILE)] = d_gate.astype(BF16)
        pre[:, pl.ds(hi, TILE)] = (act_grad * silu).astype(BF16)
        act[:, pl.ds(lo, TILE)] = (prob * activation).astype(BF16)
        total = jnp.sum(activation * raw, axis=1, keepdims=True)
        sg[...] += jnp.broadcast_to(total, sg.shape)
        return 0

    lax.fori_loop(0, HID // TILE, forward, 0, unroll=True)

    def flip_act(i, _):
        c = pl.multiple_of(i * 128, 128)
        at[pl.ds(c, 128), :] = act[:, pl.ds(c, 128)].T
        return 0

    lax.fori_loop(0, HID // 128, flip_act, 0, unroll=True)

    def backward(i, _):
        cols = pl.ds(pl.multiple_of(i * TILE, TILE), TILE)
        gin[...] = dot(xt[...], pre[:, cols], NN).astype(BF16).reshape(gin.shape)
        gout[...] = dot(at[...], dy[:, cols], NN).astype(BF16).reshape(gout.shape)
        for oj in range(4):
            for ij in range(4):
                outer = lax.rem(outer_pos + oj, 4)
                inner = lax.rem(inner_pos + ij, 4)
                b = jnp.where(first, outer * 4 + inner, inner * 4 + outer)
                held[oj, ij, 0:ROWS_IN, cols] = gin[b]
                held[oj, ij, ROWS_IN:ROWS, cols] = gout[b]
        return 0

    lax.fori_loop(0, WIDTH // TILE, backward, 0, unroll=True)

    def input_grad(i, _):
        w = w_in[i].reshape(TILE, WIDTH)
        lo = pl.multiple_of(i * TILE, TILE)
        dx[:, pl.ds(lo, TILE)] = dot(pre[...], w, NT).astype(BF16)
        return 0

    lax.fori_loop(0, WIDTH // TILE, input_grad, 0, unroll=True)


def combine_pair(p, first, pay, sel_ref, dx, sg, part):
    sel = sel_ref[p]
    at = pl.ds(pl.multiple_of(PAIR * p, PAIR), PAIR)
    rows = jnp.concatenate([dx[0, at], dx[1, at]], axis=0)
    back = dot(sel, rows, TN).astype(BF16)
    sums = jnp.concatenate([sg[0, at, 0:1], sg[1, at, 0:1]], axis=0)
    sums = sums.astype(BF16).astype(F32)
    spread = sel.astype(F32) * sums
    totals = [
        jnp.sum(spread[:PAIR], axis=0, keepdims=True),
        jnp.sum(spread[PAIR:], axis=0, keepdims=True),
    ]
    for c in range(2):
        part[c, 0:TOK] = back[c * TOK : (c + 1) * TOK]
        ids = pay[2 * p + c, 2 * TOK : 2 * TOK + TOP, 0:TOK].astype(F32)
        value = jnp.zeros((TOP, TOK), F32)
        for e in range(2):
            hit = ids == (first + e).astype(F32)
            value = value + jnp.where(hit, totals[e][:, c * TOK : (c + 1) * TOK], 0.0)
        part[c, TOK : TOK + TOP] = jnp.zeros((TOP, WIDTH), BF16)
        part[c, TOK : TOK + TOP, 0:TOK] = value.astype(BF16)


def experts_kernel(where, pay_hbm, *refs):
    pieces = refs[0:5], refs[5:10]
    grads = refs[10:15], refs[15:20]
    keep, send = refs[20:22]
    pay, x, dy, gate, sel, dx, sg, w_in, w_out, pre, act, xt, at, gin, gout, part = refs[22:38]
    held, psem, wsem, gsem, csem = refs[38:]
    first, core, iy, ix = where[0], where[1], where[2], where[3]
    loads = [
        pltpu.make_async_copy(pay_hbm.at[pl.ds(2 * p, 2)], pay.at[pl.ds(2 * p, 2)], psem.at[p])
        for p in range(CHIPS)
    ]
    for copy in loads:
        copy.start()
    weights = [
        load_weights(e, (iy, ix)[e], pieces[e], w_in.at[e], w_out.at[e], wsem.at[e])
        for e in range(2)
    ]
    upper = (
        lax.broadcasted_iota(jnp.int32, (TOK, TOK), 0)
        < lax.broadcasted_iota(jnp.int32, (TOK, TOK), 1)
    ).astype(BF16)
    slot = lax.broadcasted_iota(jnp.int32, (PAIR, TOK), 0).astype(F32)

    def pair_in(p, _):
        both = pl.ds(2 * p, 2)
        pltpu.make_async_copy(pay_hbm.at[both], pay.at[both], psem.at[p]).wait()

        @pl.when(p == START_AT)
        def _():
            for copy in weights[0]:
                copy.start()

        route_pair(p, first, pay, x, dy, gate, sel, upper, slot)
        return 0

    lax.fori_loop(0, CHIPS, pair_in, 0)

    def one(e, _):
        for n in range(10):
            src = pieces[0][(0, 0, 0, 3, 3)[n // 2]]
            rows, dst = ((pl.ds(0, ROWS_IN), w_in), (pl.ds(ROWS_IN, ROWS_OUT), w_out))[n % 2]
            inner = pl.ds(0, src.shape[0])
            pltpu.make_async_copy(src.at[:, rows], dst.at[e, 0, inner], wsem.at[e, n]).wait()

        @pl.when(e == 0)
        def _():
            for copy in weights[1]:
                copy.start()

        outer_pos = jnp.where(e == 0, iy, ix)
        inner_pos = jnp.where(e == 0, ix, iy)
        expert_step(
            e == 0, outer_pos, inner_pos, x.at[e], dy.at[e], gate.at[e], w_in.at[e], w_out.at[e],
            held.at[e], dx.at[e], sg.at[e], pre, act, xt, at, gin, gout,
        )
        for i in range(2):

            @pl.when(e == i)
            def _():
                for copy in stores_of(held.at[i], grads[i], gsem.at[i]):
                    copy.start()

        return 0

    lax.fori_loop(0, 2, one, 0)
    def sends(p):
        return [
            pltpu.make_async_copy(part.at[p, core], keep.at[p], csem.at[p, 0]),
            pltpu.make_async_copy(part.at[p, 1 - core], send.at[p], csem.at[p, 1]),
        ]

    def pair_out(p, _):
        combine_pair(p, first, pay, sel, dx, sg, part.at[p])
        for copy in sends(p):
            copy.start()
        return 0

    lax.fori_loop(0, CHIPS, pair_out, 0)
    outs = [copy for p in range(CHIPS) for copy in sends(p)]
    for e in range(2):
        outs += stores_of(held.at[e], grads[e], gsem.at[e])
    for copy in outs:
        copy.wait()


def experts(where, pay, pieces0, pieces1):
    return call(
        experts_kernel,
        "experts",
        [*[shape(4, ROWS, WIDTH)] * 3, *[shape(2, ROWS, WIDTH)] * 2] * 2
        + [pltpu.VMEM((CHIPS, TOK + TOP, WIDTH), BF16), shape(CHIPS, TOK + TOP, WIDTH)],
        where,
        pay,
        *pieces0,
        *pieces1,
        scalars=1,
        specs=[HBM] + [HBM] * 10,
        out_specs=[HBM] * 10 + [VM, HBM],
        scratch=[
            pltpu.VMEM((2 * CHIPS, 2 * TOK + TOP, WIDTH), BF16),
            pltpu.VMEM((2, SLOTS, WIDTH), BF16),
            pltpu.VMEM((2, SLOTS, WIDTH), BF16),
            pltpu.VMEM((2, SLOTS, TOK), F32),
            pltpu.VMEM((CHIPS, 2 * PAIR, 2 * TOK), BF16),
            pltpu.VMEM((2, SLOTS, WIDTH), BF16),
            pltpu.VMEM((2, SLOTS, TOK), F32),
            pltpu.VMEM((2, 4, 4, ROWS_IN, WIDTH), BF16),
            pltpu.VMEM((2, 4, 4, ROWS_OUT, WIDTH), BF16),
            pltpu.VMEM((SLOTS, WIDTH), BF16),
            pltpu.VMEM((SLOTS, HID), BF16),
            pltpu.VMEM((WIDTH, SLOTS), BF16),
            pltpu.VMEM((HID, SLOTS), BF16),
            pltpu.VMEM((16, ROWS_IN, TILE), BF16),
            pltpu.VMEM((16, ROWS_OUT, TILE), BF16),
            pltpu.VMEM((CHIPS, 2, TOK + TOP, WIDTH), BF16),
            pltpu.VMEM((2, 4, 4, ROWS, WIDTH), BF16),
            pltpu.SemaphoreType.DMA((CHIPS,)),
            pltpu.SemaphoreType.DMA((2, 10)),
            pltpu.SemaphoreType.DMA((2, 5)),
            pltpu.SemaphoreType.DMA((CHIPS, 2)),
        ],
        cost=cost(4 * 640 * 1024 * 4096, 20_000_000),
        limit=56,
    )


def add(a, b):
    return a.astype(F32) + b.astype(F32)


def fold_kernel(up, down, below, above, up_out, down_out, kept, got, sem):
    moves = (up, below, up_out, pl.ds(0, 2)), (down, above, down_out, pl.ds(2, 2))
    loads = []
    for i, (block, arrived, _, half) in enumerate(moves):
        loads.append(pltpu.make_async_copy(block.at[half], kept.at[i], sem.at[i]))
        loads.append(pltpu.make_async_copy(arrived, got.at[i], sem.at[2 + i]))
    for copy in loads:
        copy.start()
    stores = []
    for i, (_, _, out, half) in enumerate(moves):
        loads[2 * i].wait()
        loads[2 * i + 1].wait()
        kept[i] = add(kept[i], got[i]).astype(BF16)
        stores.append(pltpu.make_async_copy(kept.at[i], out.at[half], sem.at[4 + i]))
        stores[-1].start()
    for copy in stores:
        copy.wait()


def fold(up, down, below, above):
    return call(
        fold_kernel,
        "fold",
        [shape(4, ROWS, WIDTH)] * 2,
        up,
        down,
        below,
        above,
        specs=[HBM] * 4,
        out_specs=[HBM] * 2,
        scratch=[
            pltpu.VMEM((2, 2, ROWS, WIDTH), BF16),
            pltpu.VMEM((2, 2, ROWS, WIDTH), BF16),
            pltpu.SemaphoreType.DMA((6,)),
        ],
        cost=cost(0, 1024),
        input_output_aliases={0: 0, 1: 1},
    )


def join_kernel(a, b, out):
    out[...] = add(a[...], b[...]).astype(BF16)


def join(a, b):
    return call(join_kernel, "join", shape(*a.shape), a, b, cost=cost(0, 1024))


def total_kernel(own, below, above, *outs):
    for i in range(4):
        value = add(own[i], below[i]) + above[i].astype(F32)
        outs[i][...] = value if i == 0 else value.astype(BF16)


def total_of(own, below, above):
    outs = [shape(ROWS, WIDTH, dtype=F32)] + [shape(ROWS, WIDTH)] * 3
    return call(total_kernel, "total", outs, own, below, above, cost=cost(0, 1024))


def finish_kernel(*refs):
    done = refs[8]
    d_tok, d_gate, d_in, d_out = refs[9:]
    for e in range(2):
        kept, a, b, c = refs[4 * e : 4 * e + 4]
        total = kept[...] + a[...].astype(F32) + b[...].astype(F32) + c[...].astype(F32)
        d_in[e] = total[:ROWS_IN]
        d_out[e] = total[ROWS_IN:]
    d_tok[...] = done[:TOK]
    d_gate[...] = done[TOK:, :TOK]


def finish(*parts):
    return call(
        finish_kernel,
        "finish",
        [
            shape(TOK, WIDTH),
            shape(TOP, TOK),
            shape(2, ROWS_IN, WIDTH, dtype=F32),
            shape(2, ROWS_OUT, WIDTH, dtype=F32),
        ],
        *parts,
        cost=cost(0, 1024),
    )


def gather_ring(block, axis):
    half = block.shape[0] // 2
    below = lax.ppermute(block, axis, UP)
    above = lax.ppermute(block, axis, DOWN)
    far_a = lax.ppermute(below[:half], axis, UP)
    far_b = lax.ppermute(above[half:], axis, DOWN)
    return block, below, above, far_a, far_b


def gather_weights(own, index, where, inner, outer):
    below, above = swap(own, own, inner)
    across = lax.ppermute(own, inner, ACROSS)
    return gather_ring(place(index, where, own, below, across, above), outer)


def swap(a, b, axis):
    return lax.ppermute(a, axis, UP), lax.ppermute(b, axis, DOWN)


def spread(parts, axis):
    kept, up, far, down = parts
    up, down = swap(up, down, axis)
    return kept, up, lax.ppermute(far, axis, ACROSS), down


def body(tokens, cotangent, expert_ids, gate_probs, gate_up, down_proj):
    ix = lax.axis_index("x").astype(jnp.int32)
    iy = lax.axis_index("y").astype(jnp.int32)
    core = lax.axis_index("core").astype(jnp.int32)
    first = (2 * (2 * lax.axis_index("z") + core)).astype(jnp.int32)
    where, ids = lax.optimization_barrier((jnp.stack([first, core, iy, ix]), expert_ids.T))
    pay = pack(tokens, cotangent, ids, gate_probs.T)
    pay = lax.all_gather(pay, ("z", "core"), axis=0, tiled=False)
    own0, own1 = own_rows(gate_up, down_proj)
    pieces0 = gather_weights(own0, 3, where, "x", "y")
    pieces1 = gather_weights(own1, 2, where, "y", "x")

    out = experts(where, pay, pieces0, pieces1)
    mine0, up0, dn0, a0, b0 = out[:5]
    mine1, up1, dn1, a1, b1 = out[5:10]
    keep, send = out[10:]
    got = lax.ppermute(send, "core", [(0, 1), (1, 0)])
    below0, above0 = swap(a0, b0, "y")
    below1, above1 = swap(a1, b1, "x")
    below0, above0 = swap(*fold(up0, dn0, below0, above0), "y")
    below1, above1 = swap(*fold(up1, dn1, below1, above1), "x")
    pair = join(keep, got).reshape(CHIPS * (TOK + TOP), WIDTH)
    done = lax.psum_scatter(pair, "z", scatter_dimension=0, tiled=True)
    out0 = total_of(mine0, below0, above0)
    out1 = total_of(mine1, below1, above1)
    grad_tokens, grad_gates, grad_gate_up, grad_down = finish(
        *spread(out0, "x"), *spread(out1, "y"), done
    )
    return grad_tokens, grad_gates.T, grad_gate_up, grad_down


def solution(mesh):
    grid = Mesh(mesh.devices.reshape(4, 4, 8, 2), ("y", "x", "z", "core"))
    rows = P(("y", "x", "z", "core"), None)
    held = P(("z", "core"), ("y", "x"), None)
    return jax.shard_map(
        body,
        mesh=grid,
        in_specs=(rows, rows, rows, rows, held, held),
        out_specs=(rows, rows, held, held),
        check_vma=False,
    )
```

```python
import functools

import jax
import jax.numpy as jnp
from jax import lax
from jax.experimental import pallas as pl
from jax.experimental.pallas import tpu as pltpu
from jax.sharding import Mesh
from jax.sharding import PartitionSpec as P

BF16 = jnp.bfloat16
F32 = jnp.float32
TOP = 8
CAP = 40
TOK = 128
WIDTH = 1024
HID = 512
ROWS_IN = 64
ROWS_OUT = 32
ROWS = ROWS_IN + ROWS_OUT
CHIPS = 8
PAIR = 2 * CAP
SLOTS = CHIPS * PAIR
MIB = 1024 * 1024

UP = [(i, (i + 1) % 4) for i in range(4)]
DOWN = [(i, (i - 1) % 4) for i in range(4)]
ACROSS = [(i, (i + 2) % 4) for i in range(4)]


def dot(a, b, dims):
    return lax.dot_general(a, b, (dims, ((), ())), preferred_element_type=F32)


NN = ((1,), (0,))
NT = ((1,), (1,))
TN = ((0,), (0,))


def call(kernel, name, out_shape, *args, scalars=0, specs=None, out_specs=None, scratch=(), cost=None, limit=8, **more):
    vmem = pl.BlockSpec(memory_space=pltpu.VMEM)
    smem = pl.BlockSpec(memory_space=pltpu.SMEM)
    n = len(args) - scalars
    many = isinstance(out_shape, list)
    return pl.pallas_call(
        kernel,
        name=name,
        in_specs=[smem] * scalars + (specs or [vmem] * n),
        out_specs=out_specs or ([vmem] * len(out_shape) if many else vmem),
        out_shape=out_shape,
        scratch_shapes=list(scratch),
        compiler_params=pltpu.CompilerParams(vmem_limit_bytes=limit * MIB),
        cost_estimate=cost,
        **more,
    )(*args)


def cost(flops, nbytes):
    return pl.CostEstimate(flops=flops, bytes_accessed=nbytes, transcendentals=0)


def shape(*dims, dtype=BF16):
    return jax.ShapeDtypeStruct(dims, dtype)


ANY = pl.BlockSpec(memory_space=pl.ANY)
HBM = pl.BlockSpec(memory_space=pltpu.HBM)
VM = pl.BlockSpec(memory_space=pltpu.VMEM)


def pack_kernel(tok, cot, ids, probs, pay, buf, meta, sem):
    halves = [
        pltpu.make_async_copy(tok, buf.at[0], sem.at[0]),
        pltpu.make_async_copy(cot, buf.at[1], sem.at[1]),
    ]
    for copy in halves:
        copy.start()
    meta[...] = jnp.zeros_like(meta)
    meta[:, 0:TOK] = ids[...].astype(F32).astype(BF16)
    meta[:, TOK : 2 * TOK] = probs[...]
    out = [pltpu.make_async_copy(meta, pay.at[pl.ds(2 * TOK, TOP)], sem.at[2])]
    out[0].start()
    for i in range(2):
        halves[i].wait()
        out.append(pltpu.make_async_copy(buf.at[i], pay.at[pl.ds(i * TOK, TOK)], sem.at[3 + i]))
        out[-1].start()
    for copy in out:
        copy.wait()


def pack(tokens, cotangent, ids, probs):
    return call(
        pack_kernel,
        "pack",
        shape(2 * TOK + TOP, WIDTH),
        tokens,
        cotangent,
        ids,
        probs,
        specs=[HBM, HBM, VM, VM],
        out_specs=HBM,
        limit=60,
        scratch=[
            pltpu.VMEM((2, TOK, WIDTH), BF16),
            pltpu.VMEM((TOP, WIDTH), BF16),
            pltpu.SemaphoreType.DMA((5,)),
        ],
        cost=cost(0, 2_000_000),
    )


def rows_kernel(gu, dn, own0, own1):
    for e, own in enumerate((own0, own1)):
        own[0:ROWS_IN] = gu[e]
        own[ROWS_IN:ROWS] = dn[e]


def own_rows(gate_up, down_proj):
    return call(
        rows_kernel, "own_rows", [shape(ROWS, WIDTH)] * 2, gate_up, down_proj, cost=cost(0, 800_000)
    )


def place_kernel(index, me_ref, own, below, across, above, out):
    for j, block in enumerate((own, below, across, above)):
        out[lax.rem(me_ref[index] + 4 - j, 4)] = block[...]


def place(index, where, own, below, across, above):
    return call(
        functools.partial(place_kernel, index),
        "place",
        shape(4, ROWS, WIDTH),
        where,
        own,
        below,
        across,
        above,
        scalars=1,
        cost=cost(0, 1_600_000),
    )


TILE = 256
BACK_TILE = 512
START_AT = 2


def load_weights(e, outer_pos, pieces, w_in, w_out, sem):
    own, below, above, far_a, far_b = pieces
    copies = []
    for offset, lo, src in ((0, 0, own), (1, 0, below), (3, 0, above), (2, 0, far_a), (2, 2, far_b)):
        outer = lax.rem(outer_pos + 4 - offset, 4)
        inner = pl.ds(lo, src.shape[0])
        for rows, dst in ((pl.ds(0, ROWS_IN), w_in), (pl.ds(ROWS_IN, ROWS_OUT), w_out)):
            at = dst.at[outer, inner] if e == 0 else dst.at[inner, outer]
            copies.append(pltpu.make_async_copy(src.at[:, rows], at, sem.at[len(copies)]))
    return copies


def route_pair(p, first, pay, x_ref, dy_ref, gate_ref, sel_ref, upper, slot):
    named, weights = [], []
    for e in range(2):
        expert = (first + e).astype(F32)
        for c in range(2):
            part = pay[2 * p + c, 2 * TOK : 2 * TOK + TOP, 0 : 2 * TOK]
            hit = jnp.where(part[:, :TOK].astype(F32) == expert, 1.0, 0.0)
            named.append(jnp.sum(hit, axis=0, keepdims=True))
            weights.append(jnp.sum(hit * part[:, TOK:].astype(F32), axis=0, keepdims=True))
    marks = jnp.concatenate(named + named, axis=0)
    ranks = dot(marks.astype(BF16), upper, NN)
    picks = []
    for e in range(2):
        halves = []
        for c in range(2):
            i = 2 * e + c
            at = jnp.where(marks[i : i + 1] > 0.5, ranks[i : i + 1] + float(CAP * c), -1.0)
            halves.append(jnp.where(slot == at, 1.0, 0.0))
        pick = jnp.concatenate(halves, axis=1)
        prob = jnp.concatenate([weights[2 * e], weights[2 * e + 1]], axis=1)
        column = jnp.sum(pick * prob, axis=1, keepdims=True)
        gate_ref[e, pl.ds(pl.multiple_of(PAIR * p, PAIR), PAIR)] = jnp.broadcast_to(column, (PAIR, TOK))
        picks.append(pick)
    sel = jnp.concatenate(picks, axis=0).astype(BF16)
    sel_ref[p] = sel
    rows = pl.ds(pl.multiple_of(PAIR * p, PAIR), PAIR)
    for lo, out in ((0, x_ref), (TOK, dy_ref)):
        both = jnp.concatenate([pay[2 * p, lo : lo + TOK], pay[2 * p + 1, lo : lo + TOK]], axis=0)
        routed = dot(sel, both, NN).astype(BF16)
        out[0, rows] = routed[:PAIR]
        out[1, rows] = routed[PAIR:]


def stores_of(held, grads, sem):
    own, up, down, far_a, far_b = grads
    return [
        pltpu.make_async_copy(held.at[2, pl.ds(0, 2)], far_a, sem.at[0]),
        pltpu.make_async_copy(held.at[2, pl.ds(2, 2)], far_b, sem.at[1]),
        pltpu.make_async_copy(held.at[1], up, sem.at[2]),
        pltpu.make_async_copy(held.at[3], down, sem.at[3]),
        pltpu.make_async_copy(held.at[0], own, sem.at[4]),
    ]


def expert_step(
    first, outer_pos, inner_pos, x, dy, gate, w_in, w_out, held, dx, sg,
    pre, act, xt, at, gin, gout,
):
    def flip(i, _):
        c = pl.multiple_of(i * 128, 128)
        xt[pl.ds(c, 128), :] = x[:, pl.ds(c, 128)].T
        return 0

    lax.fori_loop(0, WIDTH // 128, flip, 0, unroll=True)
    sg[...] = jnp.zeros_like(sg)

    def forward(i, _):
        lo = pl.multiple_of(i * TILE, TILE)
        hi = pl.multiple_of(HID + i * TILE, TILE)
        wg = w_in[:, :, :, pl.ds(lo, TILE)].reshape(WIDTH, TILE)
        wu = w_in[:, :, :, pl.ds(hi, TILE)].reshape(WIDTH, TILE)
        wd = w_out[pl.ds(2 * i, 2)].reshape(TILE, WIDTH)
        gate_pre = dot(x[...], wg, NN)
        up_pre = dot(x[...], wu, NN)
        raw = dot(dy[...], wd, NT)
        prob = gate[:, 0:1]
        s = jax.nn.sigmoid(gate_pre)
        silu = gate_pre * s
        activation = silu * up_pre
        act_grad = prob * raw
        d_gate = act_grad * up_pre * s * (1.0 + gate_pre * (1.0 - s))
        pre[:, pl.ds(lo, TILE)] = d_gate.astype(BF16)
        pre[:, pl.ds(hi, TILE)] = (act_grad * silu).astype(BF16)
        act[:, pl.ds(lo, TILE)] = (prob * activation).astype(BF16)
        total = jnp.sum(activation * raw, axis=1, keepdims=True)
        sg[...] += jnp.broadcast_to(total, sg.shape)
        return 0

    lax.fori_loop(0, HID // TILE, forward, 0, unroll=True)

    def flip_act(i, _):
        c = pl.multiple_of(i * 128, 128)
        at[pl.ds(c, 128), :] = act[:, pl.ds(c, 128)].T
        return 0

    lax.fori_loop(0, HID // 128, flip_act, 0, unroll=True)

    def backward(i, _):
        cols = pl.ds(pl.multiple_of(i * BACK_TILE, BACK_TILE), BACK_TILE)
        gin[...] = dot(xt[...], pre[:, cols], NN).astype(BF16).reshape(gin.shape)
        gout[...] = dot(at[...], dy[:, cols], NN).astype(BF16).reshape(gout.shape)
        for oj in range(4):
            for ij in range(4):
                outer = lax.rem(outer_pos + oj, 4)
                inner = lax.rem(inner_pos + ij, 4)
                b = jnp.where(first, outer * 4 + inner, inner * 4 + outer)
                held[oj, ij, 0:ROWS_IN, cols] = gin[b]
                held[oj, ij, ROWS_IN:ROWS, cols] = gout[b]
        return 0

    lax.fori_loop(0, WIDTH // BACK_TILE, backward, 0, unroll=True)

    def input_grad(i, _):
        w = w_in[i].reshape(TILE, WIDTH)
        lo = pl.multiple_of(i * TILE, TILE)
        dx[:, pl.ds(lo, TILE)] = dot(pre[...], w, NT).astype(BF16)
        return 0

    lax.fori_loop(0, WIDTH // TILE, input_grad, 0, unroll=True)


def combine_pair(p, first, pay, sel_ref, dx, sg, part):
    sel = sel_ref[p]
    at = pl.ds(pl.multiple_of(PAIR * p, PAIR), PAIR)
    rows = jnp.concatenate([dx[0, at], dx[1, at]], axis=0)
    back = dot(sel, rows, TN).astype(BF16)
    sums = jnp.concatenate([sg[0, at, 0:1], sg[1, at, 0:1]], axis=0)
    sums = sums.astype(BF16).astype(F32)
    spread = sel.astype(F32) * sums
    totals = [
        jnp.sum(spread[:PAIR], axis=0, keepdims=True),
        jnp.sum(spread[PAIR:], axis=0, keepdims=True),
    ]
    for c in range(2):
        part[c, 0:TOK] = back[c * TOK : (c + 1) * TOK]
        ids = pay[2 * p + c, 2 * TOK : 2 * TOK + TOP, 0:TOK].astype(F32)
        value = jnp.zeros((TOP, TOK), F32)
        for e in range(2):
            hit = ids == (first + e).astype(F32)
            value = value + jnp.where(hit, totals[e][:, c * TOK : (c + 1) * TOK], 0.0)
        part[c, TOK : TOK + TOP] = jnp.zeros((TOP, WIDTH), BF16)
        part[c, TOK : TOK + TOP, 0:TOK] = value.astype(BF16)


def experts_kernel(where, pay_hbm, *refs):
    pieces = refs[0:5], refs[5:10]
    grads = refs[10:15], refs[15:20]
    keep, send = refs[20:22]
    pay, x, dy, gate, sel, dx, sg, w_in, w_out, pre, act, xt, at, gin, gout, part = refs[22:38]
    held, psem, wsem, gsem, csem = refs[38:]
    first, core, iy, ix = where[0], where[1], where[2], where[3]
    loads = [
        pltpu.make_async_copy(pay_hbm.at[pl.ds(2 * p, 2)], pay.at[pl.ds(2 * p, 2)], psem.at[p])
        for p in range(CHIPS)
    ]
    for copy in loads:
        copy.start()
    weights = [
        load_weights(e, (iy, ix)[e], pieces[e], w_in.at[e], w_out.at[e], wsem.at[e])
        for e in range(2)
    ]
    upper = (
        lax.broadcasted_iota(jnp.int32, (TOK, TOK), 0)
        < lax.broadcasted_iota(jnp.int32, (TOK, TOK), 1)
    ).astype(BF16)
    slot = lax.broadcasted_iota(jnp.int32, (PAIR, TOK), 0).astype(F32)

    def pair_in(p, _):
        both = pl.ds(2 * p, 2)
        pltpu.make_async_copy(pay_hbm.at[both], pay.at[both], psem.at[p]).wait()

        @pl.when(p == START_AT)
        def _():
            for copy in weights[0]:
                copy.start()

        route_pair(p, first, pay, x, dy, gate, sel, upper, slot)
        return 0

    lax.fori_loop(0, CHIPS, pair_in, 0)

    def one(e, _):
        for n in range(10):
            src = pieces[0][(0, 0, 0, 3, 3)[n // 2]]
            rows, dst = ((pl.ds(0, ROWS_IN), w_in), (pl.ds(ROWS_IN, ROWS_OUT), w_out))[n % 2]
            inner = pl.ds(0, src.shape[0])
            pltpu.make_async_copy(src.at[:, rows], dst.at[e, 0, inner], wsem.at[e, n]).wait()

        @pl.when(e == 0)
        def _():
            for copy in weights[1]:
                copy.start()

        outer_pos = jnp.where(e == 0, iy, ix)
        inner_pos = jnp.where(e == 0, ix, iy)
        expert_step(
            e == 0, outer_pos, inner_pos, x.at[e], dy.at[e], gate.at[e], w_in.at[e], w_out.at[e],
            held.at[e], dx.at[e], sg.at[e], pre, act, xt, at, gin, gout,
        )
        for i in range(2):

            @pl.when(e == i)
            def _():
                for copy in stores_of(held.at[i], grads[i], gsem.at[i]):
                    copy.start()

        return 0

    lax.fori_loop(0, 2, one, 0)
    def sends(p):
        return [
            pltpu.make_async_copy(part.at[p, core], keep.at[p], csem.at[p, 0]),
            pltpu.make_async_copy(part.at[p, 1 - core], send.at[p], csem.at[p, 1]),
        ]

    def pair_out(p, _):
        combine_pair(p, first, pay, sel, dx, sg, part.at[p])
        for copy in sends(p):
            copy.start()
        return 0

    lax.fori_loop(0, CHIPS, pair_out, 0)
    outs = [copy for p in range(CHIPS) for copy in sends(p)]
    for e in range(2):
        outs += stores_of(held.at[e], grads[e], gsem.at[e])
    for copy in outs:
        copy.wait()


def experts(where, pay, pieces0, pieces1):
    return call(
        experts_kernel,
        "experts",
        [*[shape(4, ROWS, WIDTH)] * 3, *[shape(2, ROWS, WIDTH)] * 2] * 2
        + [pltpu.VMEM((CHIPS, TOK + TOP, WIDTH), BF16), shape(CHIPS, TOK + TOP, WIDTH)],
        where,
        pay,
        *pieces0,
        *pieces1,
        scalars=1,
        specs=[HBM] + [HBM] * 10,
        out_specs=[HBM] * 10 + [VM, HBM],
        scratch=[
            pltpu.VMEM((2 * CHIPS, 2 * TOK + TOP, WIDTH), BF16),
            pltpu.VMEM((2, SLOTS, WIDTH), BF16),
            pltpu.VMEM((2, SLOTS, WIDTH), BF16),
            pltpu.VMEM((2, SLOTS, TOK), F32),
            pltpu.VMEM((CHIPS, 2 * PAIR, 2 * TOK), BF16),
            pltpu.VMEM((2, SLOTS, WIDTH), BF16),
            pltpu.VMEM((2, SLOTS, TOK), F32),
            pltpu.VMEM((2, 4, 4, ROWS_IN, WIDTH), BF16),
            pltpu.VMEM((2, 4, 4, ROWS_OUT, WIDTH), BF16),
            pltpu.VMEM((SLOTS, WIDTH), BF16),
            pltpu.VMEM((SLOTS, HID), BF16),
            pltpu.VMEM((WIDTH, SLOTS), BF16),
            pltpu.VMEM((HID, SLOTS), BF16),
            pltpu.VMEM((16, ROWS_IN, BACK_TILE), BF16),
            pltpu.VMEM((16, ROWS_OUT, BACK_TILE), BF16),
            pltpu.VMEM((CHIPS, 2, TOK + TOP, WIDTH), BF16),
            pltpu.VMEM((2, 4, 4, ROWS, WIDTH), BF16),
            pltpu.SemaphoreType.DMA((CHIPS,)),
            pltpu.SemaphoreType.DMA((2, 10)),
            pltpu.SemaphoreType.DMA((2, 5)),
            pltpu.SemaphoreType.DMA((CHIPS, 2)),
        ],
        cost=cost(4 * 640 * 1024 * 4096, 20_000_000),
        limit=56,
    )


def add(a, b):
    return a.astype(F32) + b.astype(F32)


def fold_kernel(up, down, below, above, up_out, down_out, kept, got, sem):
    moves = (up, below, up_out, pl.ds(0, 2)), (down, above, down_out, pl.ds(2, 2))
    loads = []
    for i, (block, arrived, _, half) in enumerate(moves):
        loads.append(pltpu.make_async_copy(block.at[half], kept.at[i], sem.at[i]))
        loads.append(pltpu.make_async_copy(arrived, got.at[i], sem.at[2 + i]))
    for copy in loads:
        copy.start()
    stores = []
    for i, (_, _, out, half) in enumerate(moves):
        loads[2 * i].wait()
        loads[2 * i + 1].wait()
        kept[i] = add(kept[i], got[i]).astype(BF16)
        stores.append(pltpu.make_async_copy(kept.at[i], out.at[half], sem.at[4 + i]))
        stores[-1].start()
    for copy in stores:
        copy.wait()


def fold(up, down, below, above):
    return call(
        fold_kernel,
        "fold",
        [shape(4, ROWS, WIDTH)] * 2,
        up,
        down,
        below,
        above,
        specs=[HBM] * 4,
        out_specs=[HBM] * 2,
        scratch=[
            pltpu.VMEM((2, 2, ROWS, WIDTH), BF16),
            pltpu.VMEM((2, 2, ROWS, WIDTH), BF16),
            pltpu.SemaphoreType.DMA((6,)),
        ],
        cost=cost(0, 1024),
        input_output_aliases={0: 0, 1: 1},
    )


def join_kernel(a, b, out):
    out[...] = add(a[...], b[...]).astype(BF16)


def join(a, b):
    return call(join_kernel, "join", shape(*a.shape), a, b, cost=cost(0, 1024))


def total_kernel(own, below, above, *outs):
    for i in range(4):
        value = add(own[i], below[i]) + above[i].astype(F32)
        outs[i][...] = value if i == 0 else value.astype(BF16)


def total_of(own, below, above):
    outs = [shape(ROWS, WIDTH, dtype=F32)] + [shape(ROWS, WIDTH)] * 3
    return call(total_kernel, "total", outs, own, below, above, cost=cost(0, 1024))


def tokens_kernel(done, d_tok, d_gate):
    d_tok[...] = done[:TOK]
    d_gate[...] = done[TOK:, :TOK]


def tokens_of(done):
    return call(
        tokens_kernel, "tokens", [shape(TOK, WIDTH), shape(TOP, TOK)], done, cost=cost(0, 1024)
    )


def finish_kernel(*refs):
    d_in, d_out = refs[8:]
    for e in range(2):
        kept, a, b, c = refs[4 * e : 4 * e + 4]
        total = kept[...] + a[...].astype(F32) + b[...].astype(F32) + c[...].astype(F32)
        d_in[e] = total[:ROWS_IN]
        d_out[e] = total[ROWS_IN:]


def finish(*parts):
    return call(
        finish_kernel,
        "finish",
        [shape(2, ROWS_IN, WIDTH, dtype=F32), shape(2, ROWS_OUT, WIDTH, dtype=F32)],
        *parts,
        cost=cost(0, 1024),
    )


def gather_ring(block, axis):
    half = block.shape[0] // 2
    below = lax.ppermute(block, axis, UP)
    above = lax.ppermute(block, axis, DOWN)
    far_a = lax.ppermute(below[:half], axis, UP)
    far_b = lax.ppermute(above[half:], axis, DOWN)
    return block, below, above, far_a, far_b


def gather_weights(own, index, where, inner, outer):
    below, above = swap(own, own, inner)
    across = lax.ppermute(own, inner, ACROSS)
    return gather_ring(place(index, where, own, below, across, above), outer)


def swap(a, b, axis):
    return lax.ppermute(a, axis, UP), lax.ppermute(b, axis, DOWN)


def spread(parts, axis):
    kept, up, far, down = parts
    up, down = swap(up, down, axis)
    return kept, up, lax.ppermute(far, axis, ACROSS), down


def body(tokens, cotangent, expert_ids, gate_probs, gate_up, down_proj):
    ix = lax.axis_index("x").astype(jnp.int32)
    iy = lax.axis_index("y").astype(jnp.int32)
    core = lax.axis_index("core").astype(jnp.int32)
    first = (2 * (2 * lax.axis_index("z") + core)).astype(jnp.int32)
    where, ids = lax.optimization_barrier((jnp.stack([first, core, iy, ix]), expert_ids.T))
    pay = pack(tokens, cotangent, ids, gate_probs.T)
    pay = lax.all_gather(pay, ("z", "core"), axis=0, tiled=False)
    own0, own1 = own_rows(gate_up, down_proj)
    pieces0 = gather_weights(own0, 3, where, "x", "y")
    pieces1 = gather_weights(own1, 2, where, "y", "x")

    out = experts(where, pay, pieces0, pieces1)
    mine0, up0, dn0, a0, b0 = out[:5]
    mine1, up1, dn1, a1, b1 = out[5:10]
    keep, send = out[10:]
    got = lax.ppermute(send, "core", [(0, 1), (1, 0)])
    below0, above0 = swap(a0, b0, "y")
    below1, above1 = swap(a1, b1, "x")
    below0, above0 = swap(*fold(up0, dn0, below0, above0), "y")
    below1, above1 = swap(*fold(up1, dn1, below1, above1), "x")
    pair = join(keep, got).reshape(CHIPS * (TOK + TOP), WIDTH)
    done = lax.psum_scatter(pair, "z", scatter_dimension=0, tiled=True)
    out0 = total_of(mine0, below0, above0)
    out1 = total_of(mine1, below1, above1)
    grad_tokens, grad_gates = tokens_of(done)
    parts0 = spread(out0, "x")
    kept0, grad_tokens, grad_gates = lax.optimization_barrier(
        (parts0[0], grad_tokens, grad_gates)
    )
    grad_gate_up, grad_down = finish(kept0, *parts0[1:], *spread(out1, "y"))
    return grad_tokens, grad_gates.T, grad_gate_up, grad_down


def solution(mesh):
    grid = Mesh(mesh.devices.reshape(4, 4, 8, 2), ("y", "x", "z", "core"))
    rows = P(("y", "x", "z", "core"), None)
    held = P(("z", "core"), ("y", "x"), None)
    return jax.shard_map(
        body,
        mesh=grid,
        in_specs=(rows, rows, rows, rows, held, held),
        out_specs=(rows, rows, held, held),
        check_vma=False,
    )
```

```python
import functools

import jax
import jax.numpy as jnp
from jax import lax
from jax.experimental import pallas as pl
from jax.experimental.pallas import tpu as pltpu
from jax.sharding import Mesh
from jax.sharding import PartitionSpec as P

BF16 = jnp.bfloat16
F32 = jnp.float32
TOP = 8
CAP = 40
TOK = 128
WIDTH = 1024
HID = 512
ROWS_IN = 64
ROWS_OUT = 32
ROWS = ROWS_IN + ROWS_OUT
CHIPS = 8
PAIR = 2 * CAP
SLOTS = CHIPS * PAIR
MIB = 1024 * 1024

UP = [(i, (i + 1) % 4) for i in range(4)]
DOWN = [(i, (i - 1) % 4) for i in range(4)]
ACROSS = [(i, (i + 2) % 4) for i in range(4)]


def dot(a, b, dims):
    return lax.dot_general(a, b, (dims, ((), ())), preferred_element_type=F32)


NN = ((1,), (0,))
NT = ((1,), (1,))
TN = ((0,), (0,))


def call(kernel, name, out_shape, *args, scalars=0, specs=None, out_specs=None, scratch=(), cost=None, limit=8, **more):
    vmem = pl.BlockSpec(memory_space=pltpu.VMEM)
    smem = pl.BlockSpec(memory_space=pltpu.SMEM)
    n = len(args) - scalars
    many = isinstance(out_shape, list)
    return pl.pallas_call(
        kernel,
        name=name,
        in_specs=[smem] * scalars + (specs or [vmem] * n),
        out_specs=out_specs or ([vmem] * len(out_shape) if many else vmem),
        out_shape=out_shape,
        scratch_shapes=list(scratch),
        compiler_params=pltpu.CompilerParams(vmem_limit_bytes=limit * MIB),
        cost_estimate=cost,
        **more,
    )(*args)


def cost(flops, nbytes):
    return pl.CostEstimate(flops=flops, bytes_accessed=nbytes, transcendentals=0)


def shape(*dims, dtype=BF16):
    return jax.ShapeDtypeStruct(dims, dtype)


ANY = pl.BlockSpec(memory_space=pl.ANY)
HBM = pl.BlockSpec(memory_space=pltpu.HBM)
VM = pl.BlockSpec(memory_space=pltpu.VMEM)


def pack_kernel(tok, cot, ids, probs, pay, buf, meta, sem):
    halves = [
        pltpu.make_async_copy(tok, buf.at[0], sem.at[0]),
        pltpu.make_async_copy(cot, buf.at[1], sem.at[1]),
    ]
    for copy in halves:
        copy.start()
    meta[...] = jnp.zeros_like(meta)
    meta[:, 0:TOK] = ids[...].astype(F32).astype(BF16)
    meta[:, TOK : 2 * TOK] = probs[...]
    out = [pltpu.make_async_copy(meta, pay.at[pl.ds(2 * TOK, TOP)], sem.at[2])]
    out[0].start()
    for i in range(2):
        halves[i].wait()
        out.append(pltpu.make_async_copy(buf.at[i], pay.at[pl.ds(i * TOK, TOK)], sem.at[3 + i]))
        out[-1].start()
    for copy in out:
        copy.wait()


def pack(tokens, cotangent, ids, probs):
    return call(
        pack_kernel,
        "pack",
        shape(2 * TOK + TOP, WIDTH),
        tokens,
        cotangent,
        ids,
        probs,
        specs=[HBM, HBM, VM, VM],
        out_specs=HBM,
        limit=60,
        scratch=[
            pltpu.VMEM((2, TOK, WIDTH), BF16),
            pltpu.VMEM((TOP, WIDTH), BF16),
            pltpu.SemaphoreType.DMA((5,)),
        ],
        cost=cost(0, 2_000_000),
    )


def rows_kernel(gu, dn, own0, own1):
    for e, own in enumerate((own0, own1)):
        own[0:ROWS_IN] = gu[e]
        own[ROWS_IN:ROWS] = dn[e]


def own_rows(gate_up, down_proj):
    return call(
        rows_kernel, "own_rows", [shape(ROWS, WIDTH)] * 2, gate_up, down_proj, cost=cost(0, 800_000)
    )


def place_kernel(index, me_ref, own, below, across, above, out):
    for j, block in enumerate((own, below, across, above)):
        out[lax.rem(me_ref[index] + 4 - j, 4)] = block[...]


def place(index, where, own, below, across, above):
    return call(
        functools.partial(place_kernel, index),
        "place",
        shape(4, ROWS, WIDTH),
        where,
        own,
        below,
        across,
        above,
        scalars=1,
        cost=cost(0, 1_600_000),
    )


TILE = 256
BACK_TILE = 1024
START_AT = 2


def load_weights(e, outer_pos, pieces, w_in, w_out, sem):
    own, below, above, far_a, far_b = pieces
    copies = []
    for offset, lo, src in ((0, 0, own), (1, 0, below), (3, 0, above), (2, 0, far_a), (2, 2, far_b)):
        outer = lax.rem(outer_pos + 4 - offset, 4)
        inner = pl.ds(lo, src.shape[0])
        for rows, dst in ((pl.ds(0, ROWS_IN), w_in), (pl.ds(ROWS_IN, ROWS_OUT), w_out)):
            at = dst.at[outer, inner] if e == 0 else dst.at[inner, outer]
            copies.append(pltpu.make_async_copy(src.at[:, rows], at, sem.at[len(copies)]))
    return copies


def route_pair(p, first, pay, x_ref, dy_ref, gate_ref, sel_ref, upper, slot):
    named, weights = [], []
    for e in range(2):
        expert = (first + e).astype(F32)
        for c in range(2):
            part = pay[2 * p + c, 2 * TOK : 2 * TOK + TOP, 0 : 2 * TOK]
            hit = jnp.where(part[:, :TOK].astype(F32) == expert, 1.0, 0.0)
            named.append(jnp.sum(hit, axis=0, keepdims=True))
            weights.append(jnp.sum(hit * part[:, TOK:].astype(F32), axis=0, keepdims=True))
    marks = jnp.concatenate(named + named, axis=0)
    ranks = dot(marks.astype(BF16), upper, NN)
    picks = []
    for e in range(2):
        halves = []
        for c in range(2):
            i = 2 * e + c
            at = jnp.where(marks[i : i + 1] > 0.5, ranks[i : i + 1] + float(CAP * c), -1.0)
            halves.append(jnp.where(slot == at, 1.0, 0.0))
        pick = jnp.concatenate(halves, axis=1)
        prob = jnp.concatenate([weights[2 * e], weights[2 * e + 1]], axis=1)
        column = jnp.sum(pick * prob, axis=1, keepdims=True)
        gate_ref[e, pl.ds(pl.multiple_of(PAIR * p, PAIR), PAIR)] = jnp.broadcast_to(column, (PAIR, TOK))
        picks.append(pick)
    sel = jnp.concatenate(picks, axis=0).astype(BF16)
    sel_ref[p] = sel
    rows = pl.ds(pl.multiple_of(PAIR * p, PAIR), PAIR)
    for lo, out in ((0, x_ref), (TOK, dy_ref)):
        both = jnp.concatenate([pay[2 * p, lo : lo + TOK], pay[2 * p + 1, lo : lo + TOK]], axis=0)
        routed = dot(sel, both, NN).astype(BF16)
        out[0, rows] = routed[:PAIR]
        out[1, rows] = routed[PAIR:]


def stores_of(held, grads, sem):
    own, up, down, far_a, far_b = grads
    return [
        pltpu.make_async_copy(held.at[2, pl.ds(0, 2)], far_a, sem.at[0]),
        pltpu.make_async_copy(held.at[2, pl.ds(2, 2)], far_b, sem.at[1]),
        pltpu.make_async_copy(held.at[1], up, sem.at[2]),
        pltpu.make_async_copy(held.at[3], down, sem.at[3]),
        pltpu.make_async_copy(held.at[0], own, sem.at[4]),
    ]


def expert_step(
    first, outer_pos, inner_pos, x, dy, gate, w_in, w_out, held, dx, sg,
    pre, act, xt, at, gin, gout,
):
    def flip(i, _):
        c = pl.multiple_of(i * 128, 128)
        xt[pl.ds(c, 128), :] = x[:, pl.ds(c, 128)].T
        return 0

    lax.fori_loop(0, WIDTH // 128, flip, 0, unroll=True)
    sg[...] = jnp.zeros_like(sg)

    def forward(i, _):
        lo = pl.multiple_of(i * TILE, TILE)
        hi = pl.multiple_of(HID + i * TILE, TILE)
        wg = w_in[:, :, :, pl.ds(lo, TILE)].reshape(WIDTH, TILE)
        wu = w_in[:, :, :, pl.ds(hi, TILE)].reshape(WIDTH, TILE)
        wd = w_out[pl.ds(2 * i, 2)].reshape(TILE, WIDTH)
        gate_pre = dot(x[...], wg, NN)
        up_pre = dot(x[...], wu, NN)
        raw = dot(dy[...], wd, NT)
        prob = gate[:, 0:1]
        s = jax.nn.sigmoid(gate_pre)
        silu = gate_pre * s
        activation = silu * up_pre
        act_grad = prob * raw
        d_gate = act_grad * up_pre * s * (1.0 + gate_pre * (1.0 - s))
        pre[:, pl.ds(lo, TILE)] = d_gate.astype(BF16)
        pre[:, pl.ds(hi, TILE)] = (act_grad * silu).astype(BF16)
        act[:, pl.ds(lo, TILE)] = (prob * activation).astype(BF16)
        total = jnp.sum(activation * raw, axis=1, keepdims=True)
        sg[...] += jnp.broadcast_to(total, sg.shape)
        return 0

    lax.fori_loop(0, HID // TILE, forward, 0, unroll=True)

    def flip_act(i, _):
        c = pl.multiple_of(i * 128, 128)
        at[pl.ds(c, 128), :] = act[:, pl.ds(c, 128)].T
        return 0

    lax.fori_loop(0, HID // 128, flip_act, 0, unroll=True)

    def backward(i, _):
        cols = pl.ds(pl.multiple_of(i * BACK_TILE, BACK_TILE), BACK_TILE)
        gin[...] = dot(xt[...], pre[:, cols], NN).astype(BF16).reshape(gin.shape)
        gout[...] = dot(at[...], dy[:, cols], NN).astype(BF16).reshape(gout.shape)
        for oj in range(4):
            for ij in range(4):
                outer = lax.rem(outer_pos + oj, 4)
                inner = lax.rem(inner_pos + ij, 4)
                b = jnp.where(first, outer * 4 + inner, inner * 4 + outer)
                held[oj, ij, 0:ROWS_IN, cols] = gin[b]
                held[oj, ij, ROWS_IN:ROWS, cols] = gout[b]
        return 0

    lax.fori_loop(0, WIDTH // BACK_TILE, backward, 0, unroll=True)

    def input_grad(i, _):
        w = w_in[i].reshape(TILE, WIDTH)
        lo = pl.multiple_of(i * TILE, TILE)
        dx[:, pl.ds(lo, TILE)] = dot(pre[...], w, NT).astype(BF16)
        return 0

    lax.fori_loop(0, WIDTH // TILE, input_grad, 0, unroll=True)


def combine_pair(p, first, pay, sel_ref, dx, sg, part):
    sel = sel_ref[p]
    at = pl.ds(pl.multiple_of(PAIR * p, PAIR), PAIR)
    rows = jnp.concatenate([dx[0, at], dx[1, at]], axis=0)
    back = dot(sel, rows, TN).astype(BF16)
    sums = jnp.concatenate([sg[0, at, 0:1], sg[1, at, 0:1]], axis=0)
    sums = sums.astype(BF16).astype(F32)
    spread = sel.astype(F32) * sums
    totals = [
        jnp.sum(spread[:PAIR], axis=0, keepdims=True),
        jnp.sum(spread[PAIR:], axis=0, keepdims=True),
    ]
    for c in range(2):
        part[c, 0:TOK] = back[c * TOK : (c + 1) * TOK]
        ids = pay[2 * p + c, 2 * TOK : 2 * TOK + TOP, 0:TOK].astype(F32)
        value = jnp.zeros((TOP, TOK), F32)
        for e in range(2):
            hit = ids == (first + e).astype(F32)
            value = value + jnp.where(hit, totals[e][:, c * TOK : (c + 1) * TOK], 0.0)
        part[c, TOK : TOK + TOP] = jnp.zeros((TOP, WIDTH), BF16)
        part[c, TOK : TOK + TOP, 0:TOK] = value.astype(BF16)


def experts_kernel(where, pay_hbm, *refs):
    pieces = refs[0:5], refs[5:10]
    grads = refs[10:15], refs[15:20]
    keep, send = refs[20:22]
    pay, x, dy, gate, sel, dx, sg, w_in, w_out, pre, act, xt, at, gin, gout, part = refs[22:38]
    held, psem, wsem, gsem, csem = refs[38:]
    first, core, iy, ix = where[0], where[1], where[2], where[3]
    loads = [
        pltpu.make_async_copy(pay_hbm.at[pl.ds(2 * p, 2)], pay.at[pl.ds(2 * p, 2)], psem.at[p])
        for p in range(CHIPS)
    ]
    for copy in loads:
        copy.start()
    weights = [
        load_weights(e, (iy, ix)[e], pieces[e], w_in.at[e], w_out.at[e], wsem.at[e])
        for e in range(2)
    ]
    upper = (
        lax.broadcasted_iota(jnp.int32, (TOK, TOK), 0)
        < lax.broadcasted_iota(jnp.int32, (TOK, TOK), 1)
    ).astype(BF16)
    slot = lax.broadcasted_iota(jnp.int32, (PAIR, TOK), 0).astype(F32)

    def pair_in(p, _):
        both = pl.ds(2 * p, 2)
        pltpu.make_async_copy(pay_hbm.at[both], pay.at[both], psem.at[p]).wait()

        @pl.when(p == START_AT)
        def _():
            for copy in weights[0]:
                copy.start()

        route_pair(p, first, pay, x, dy, gate, sel, upper, slot)
        return 0

    lax.fori_loop(0, CHIPS, pair_in, 0, unroll=2)

    def one(e, _):
        for n in range(10):
            src = pieces[0][(0, 0, 0, 3, 3)[n // 2]]
            rows, dst = ((pl.ds(0, ROWS_IN), w_in), (pl.ds(ROWS_IN, ROWS_OUT), w_out))[n % 2]
            inner = pl.ds(0, src.shape[0])
            pltpu.make_async_copy(src.at[:, rows], dst.at[e, 0, inner], wsem.at[e, n]).wait()

        @pl.when(e == 0)
        def _():
            for copy in weights[1]:
                copy.start()

        outer_pos = jnp.where(e == 0, iy, ix)
        inner_pos = jnp.where(e == 0, ix, iy)
        expert_step(
            e == 0, outer_pos, inner_pos, x.at[e], dy.at[e], gate.at[e], w_in.at[e], w_out.at[e],
            held.at[e], dx.at[e], sg.at[e], pre, act, xt, at, gin, gout,
        )
        for i in range(2):

            @pl.when(e == i)
            def _():
                for copy in stores_of(held.at[i], grads[i], gsem.at[i]):
                    copy.start()

        return 0

    lax.fori_loop(0, 2, one, 0)
    def sends(p):
        return [
            pltpu.make_async_copy(part.at[p, core], keep.at[p], csem.at[p, 0]),
            pltpu.make_async_copy(part.at[p, 1 - core], send.at[p], csem.at[p, 1]),
        ]

    def pair_out(p, _):
        combine_pair(p, first, pay, sel, dx, sg, part.at[p])
        for copy in sends(p):
            copy.start()
        return 0

    lax.fori_loop(0, CHIPS, pair_out, 0, unroll=2)
    outs = [copy for p in range(CHIPS) for copy in sends(p)]
    for e in range(2):
        outs += stores_of(held.at[e], grads[e], gsem.at[e])
    for copy in outs:
        copy.wait()


def experts(where, pay, pieces0, pieces1):
    return call(
        experts_kernel,
        "experts",
        [*[shape(4, ROWS, WIDTH)] * 3, *[shape(2, ROWS, WIDTH)] * 2] * 2
        + [pltpu.VMEM((CHIPS, TOK + TOP, WIDTH), BF16), shape(CHIPS, TOK + TOP, WIDTH)],
        where,
        pay,
        *pieces0,
        *pieces1,
        scalars=1,
        specs=[HBM] + [HBM] * 10,
        out_specs=[HBM] * 10 + [VM, HBM],
        scratch=[
            pltpu.VMEM((2 * CHIPS, 2 * TOK + TOP, WIDTH), BF16),
            pltpu.VMEM((2, SLOTS, WIDTH), BF16),
            pltpu.VMEM((2, SLOTS, WIDTH), BF16),
            pltpu.VMEM((2, SLOTS, TOK), F32),
            pltpu.VMEM((CHIPS, 2 * PAIR, 2 * TOK), BF16),
            pltpu.VMEM((2, SLOTS, WIDTH), BF16),
            pltpu.VMEM((2, SLOTS, TOK), F32),
            pltpu.VMEM((2, 4, 4, ROWS_IN, WIDTH), BF16),
            pltpu.VMEM((2, 4, 4, ROWS_OUT, WIDTH), BF16),
            pltpu.VMEM((SLOTS, WIDTH), BF16),
            pltpu.VMEM((SLOTS, HID), BF16),
            pltpu.VMEM((WIDTH, SLOTS), BF16),
            pltpu.VMEM((HID, SLOTS), BF16),
            pltpu.VMEM((16, ROWS_IN, BACK_TILE), BF16),
            pltpu.VMEM((16, ROWS_OUT, BACK_TILE), BF16),
            pltpu.VMEM((CHIPS, 2, TOK + TOP, WIDTH), BF16),
            pltpu.VMEM((2, 4, 4, ROWS, WIDTH), BF16),
            pltpu.SemaphoreType.DMA((CHIPS,)),
            pltpu.SemaphoreType.DMA((2, 10)),
            pltpu.SemaphoreType.DMA((2, 5)),
            pltpu.SemaphoreType.DMA((CHIPS, 2)),
        ],
        cost=cost(4 * 640 * 1024 * 4096, 20_000_000),
        limit=56,
    )


def add(a, b):
    return a.astype(F32) + b.astype(F32)


def fold_kernel(up, down, below, above, up_out, down_out, kept, got, sem):
    moves = (up, below, up_out, pl.ds(0, 2)), (down, above, down_out, pl.ds(2, 2))
    loads = []
    for i, (block, arrived, _, half) in enumerate(moves):
        loads.append(pltpu.make_async_copy(block.at[half], kept.at[i], sem.at[i]))
        loads.append(pltpu.make_async_copy(arrived, got.at[i], sem.at[2 + i]))
    for copy in loads:
        copy.start()
    stores = []
    for i, (_, _, out, half) in enumerate(moves):
        loads[2 * i].wait()
        loads[2 * i + 1].wait()
        kept[i] = add(kept[i], got[i]).astype(BF16)
        stores.append(pltpu.make_async_copy(kept.at[i], out.at[half], sem.at[4 + i]))
        stores[-1].start()
    for copy in stores:
        copy.wait()


def fold(up, down, below, above):
    return call(
        fold_kernel,
        "fold",
        [shape(4, ROWS, WIDTH)] * 2,
        up,
        down,
        below,
        above,
        specs=[HBM] * 4,
        out_specs=[HBM] * 2,
        scratch=[
            pltpu.VMEM((2, 2, ROWS, WIDTH), BF16),
            pltpu.VMEM((2, 2, ROWS, WIDTH), BF16),
            pltpu.SemaphoreType.DMA((6,)),
        ],
        cost=cost(0, 1024),
        input_output_aliases={0: 0, 1: 1},
    )


def join_kernel(a, b, out):
    out[...] = add(a[...], b[...]).astype(BF16)


def join(a, b):
    return call(join_kernel, "join", shape(*a.shape), a, b, cost=cost(0, 1024))


def total_kernel(own, below, above, *outs):
    for i in range(4):
        value = add(own[i], below[i]) + above[i].astype(F32)
        outs[i][...] = value if i == 0 else value.astype(BF16)


def total_of(own, below, above):
    outs = [shape(ROWS, WIDTH, dtype=F32)] + [shape(ROWS, WIDTH)] * 3
    return call(total_kernel, "total", outs, own, below, above, cost=cost(0, 1024))


def tokens_kernel(done, d_tok, d_gate):
    d_tok[...] = done[:TOK]
    d_gate[...] = done[TOK:, :TOK]


def tokens_of(done):
    return call(
        tokens_kernel, "tokens", [shape(TOK, WIDTH), shape(TOP, TOK)], done, cost=cost(0, 1024)
    )


def finish_kernel(*refs):
    d_in, d_out = refs[8:]
    for e in range(2):
        kept, a, b, c = refs[4 * e : 4 * e + 4]
        total = kept[...] + a[...].astype(F32) + b[...].astype(F32) + c[...].astype(F32)
        d_in[e] = total[:ROWS_IN]
        d_out[e] = total[ROWS_IN:]


def finish(*parts):
    return call(
        finish_kernel,
        "finish",
        [shape(2, ROWS_IN, WIDTH, dtype=F32), shape(2, ROWS_OUT, WIDTH, dtype=F32)],
        *parts,
        cost=cost(0, 1024),
    )


def gather_ring(block, axis):
    half = block.shape[0] // 2
    below = lax.ppermute(block, axis, UP)
    above = lax.ppermute(block, axis, DOWN)
    far_a = lax.ppermute(below[:half], axis, UP)
    far_b = lax.ppermute(above[half:], axis, DOWN)
    return block, below, above, far_a, far_b


def gather_weights(own, index, where, inner, outer):
    below, above = swap(own, own, inner)
    across = lax.ppermute(own, inner, ACROSS)
    return gather_ring(place(index, where, own, below, across, above), outer)


def swap(a, b, axis):
    return lax.ppermute(a, axis, UP), lax.ppermute(b, axis, DOWN)


def spread(parts, axis):
    kept, up, far, down = parts
    up, down = swap(up, down, axis)
    return kept, up, lax.ppermute(far, axis, ACROSS), down


def body(tokens, cotangent, expert_ids, gate_probs, gate_up, down_proj):
    ix = lax.axis_index("x").astype(jnp.int32)
    iy = lax.axis_index("y").astype(jnp.int32)
    core = lax.axis_index("core").astype(jnp.int32)
    first = (2 * (2 * lax.axis_index("z") + core)).astype(jnp.int32)
    where, ids = lax.optimization_barrier((jnp.stack([first, core, iy, ix]), expert_ids.T))
    pay = pack(tokens, cotangent, ids, gate_probs.T)
    pay = lax.all_gather(pay, ("z", "core"), axis=0, tiled=False)
    own0, own1 = own_rows(gate_up, down_proj)
    pieces0 = gather_weights(own0, 3, where, "x", "y")
    pieces1 = gather_weights(own1, 2, where, "y", "x")

    out = experts(where, pay, pieces0, pieces1)
    mine0, up0, dn0, a0, b0 = out[:5]
    mine1, up1, dn1, a1, b1 = out[5:10]
    keep, send = out[10:]
    got = lax.ppermute(send, "core", [(0, 1), (1, 0)])
    below0, above0 = swap(a0, b0, "y")
    below1, above1 = swap(a1, b1, "x")
    below0, above0 = swap(*fold(up0, dn0, below0, above0), "y")
    below1, above1 = swap(*fold(up1, dn1, below1, above1), "x")
    pair = join(keep, got).reshape(CHIPS * (TOK + TOP), WIDTH)
    done = lax.psum_scatter(pair, "z", scatter_dimension=0, tiled=True)
    out0 = total_of(mine0, below0, above0)
    out1 = total_of(mine1, below1, above1)
    grad_tokens, grad_gates = tokens_of(done)
    parts0 = spread(out0, "x")
    kept0, grad_tokens, grad_gates = lax.optimization_barrier(
        (parts0[0], grad_tokens, grad_gates)
    )
    grad_gate_up, grad_down = finish(kept0, *parts0[1:], *spread(out1, "y"))
    return grad_tokens, grad_gates.T, grad_gate_up, grad_down


def solution(mesh):
    grid = Mesh(mesh.devices.reshape(4, 4, 8, 2), ("y", "x", "z", "core"))
    rows = P(("y", "x", "z", "core"), None)
    held = P(("z", "core"), ("y", "x"), None)
    return jax.shard_map(
        body,
        mesh=grid,
        in_specs=(rows, rows, rows, rows, held, held),
        out_specs=(rows, rows, held, held),
        check_vma=False,
    )
```
